128 devices in a mesh: dp: 8 (over z, core), mp: 16 (over x, y).
Axes of the slice: x: 4, y: 4, z: 4, core: 2. Of those that a mesh axis runs over, the one named last changes fastest.
Arguments:
- activations: bfloat16 [16384, 5120], P(('dp', 'mp')), may hold values from -10 to 10
- cotangent: bfloat16 [16384, 5120], P('dp', 'mp'), may hold values from -1 to 1
- master_weights: float32 [5120, 5120], P('dp', 'mp'), may hold values from -32 to 32
- first_moment: float32 [5120, 5120], P('dp', 'mp'), may hold values from -1 to 1
- second_moment: float32 [5120, 5120], P('dp', 'mp'), may hold values from 0.25 to 4
- step_count: int32 [1], replicated, may hold values from 1 to 23
- language_ids: int32 [1], replicated, may hold values from 0 to 7
- language_rates: float32 [8], replicated, may hold values from 0.25 to 2
Outputs:
- new_master: float32 [5120, 5120], P('dp', 'mp')
- new_first: float32 [5120, 5120], P('dp', 'mp')
- new_second: float32 [5120, 5120], P('dp', 'mp')
- new_weights: bfloat16 [5120, 5120], P(None, 'mp')
The draws below stay inside these ranges and needn't reach their ends.
All inputs are finite; a program needn't handle non-finite values.
Results may differ from the reference program's by a relative error of at most 0.0004.
Values may be sent and summed in bfloat16 or wider, within the bound.
No kernel may reach another device: no remote copies, remote signals or barrier semaphores. Data moves between devices by JAX's collectives and lax.ppermute only.
A program may use at most 128 MiB of HBM per device.

```python
import math
import jax
import jax.numpy as jnp
from jax import lax

D = 5120
LANGS = 8
TOK_DEV = 128
TOKENS = 16384


def shared_factors(key):
    base = jax.random.fold_in(key, 7)
    key_tok, key_row, key_col = jax.random.split(base, 3)
    tok_factor = jax.random.uniform(key_tok, (TOKENS,), jnp.float32, -1.0, 1.0)
    row_factor = jax.random.uniform(key_row, (D,), jnp.float32, -1.0, 1.0)
    col_factor = jax.random.uniform(key_col, (D,), jnp.float32, -1.0, 1.0)
    return (tok_factor, row_factor, col_factor)


def draw_activations(key, part):
    tok_factor, row_factor, col_factor = shared_factors(key)
    key_noise, key_pair = jax.random.split(jax.random.fold_in(key, 11), 2)
    noise = jnp.clip(jax.random.normal(key_noise, (TOKENS, D), dtype=jnp.float32), -3.0, 3.0)
    block_count = TOKENS // TOK_DEV
    pairing = jax.random.randint(key_pair, (block_count,), 0, 8)
    tok_block = jnp.arange(TOKENS, dtype=jnp.int32) // TOK_DEV
    feat_block = jnp.arange(D, dtype=jnp.int32) * 8 // D
    spiked = pairing[tok_block][:, None] == feat_block[None, :]
    spike = jnp.where(spiked, jnp.float32(3.0), jnp.float32(1.0))
    values = noise * spike + 0.5 * tok_factor[:, None] * row_factor[None, :]
    return values.astype(jnp.bfloat16)


def draw_cotangent(key, part):
    tok_factor, row_factor, col_factor = shared_factors(key)
    key_noise = jax.random.fold_in(key, 13)
    noise = jnp.clip(jax.random.normal(key_noise, (TOKENS, D), dtype=jnp.float32), -4.0, 4.0) / jnp.sqrt(jnp.float32(TOKENS))
    coherent = 36.0 / TOKENS * tok_factor[:, None] * col_factor[None, :]
    return jnp.clip(noise + coherent, -1.0, 1.0).astype(jnp.bfloat16)


def draw_first_moment(key, part):
    tok_factor, row_factor, col_factor = shared_factors(key)
    key_noise = jax.random.fold_in(key, 17)
    noise = jnp.clip(jax.random.normal(key_noise, (D, D), dtype=jnp.float32), -4.0, 4.0) * 0.06
    return (noise + 0.3 * row_factor[:, None] * col_factor[None, :]).astype(jnp.float32)


def draw_master_weights(key, part):
    key_base, key_cols, key_rows = jax.random.split(key, 3)
    column_pos = jnp.arange(D, dtype=jnp.float32) / D
    row_pos = (jnp.arange(D, dtype=jnp.float32) / D).reshape(D, 1)
    column_scale = jnp.exp(jnp.log(3.0) * column_pos) * jnp.exp(jnp.log(3.0) * jax.random.uniform(key_cols, (D,), dtype=jnp.float32))
    base = jnp.clip(jax.random.normal(key_base, (D, D), dtype=jnp.float32), -5.0, 5.0)
    row_scale = jnp.exp(jnp.log(10.0) * row_pos) * jnp.exp(jnp.log(1.6) * jax.random.uniform(key_rows, (D, 1), dtype=jnp.float32))
    return (base * row_scale * column_scale[None, :] * 0.04).astype(jnp.float32)


def levels(rng, dims, shards, low, top_value):
    factor_of, own = 1.0, jax.random.fold_in(rng, 6)
    for dim, shards_of in shards:
        draws = jnp.exp(jax.random.uniform(jax.random.fold_in(own, dim), (shards_of,), jnp.float32, low / len(shards), top_value / len(shards)))
        factor_of = factor_of * jnp.repeat(draws, dims[dim] // shards_of).reshape([-1 if axis == dim else 1 for axis in range(len(dims))])
    return factor_of


def setup_inputs(seed: int = 0) -> dict:
    streams_of = jax.random.split(jax.random.key(seed), 9)
    return {
        "activations": draw_activations(jax.random.fold_in(streams_of[8], 71), 0),
        "cotangent": draw_cotangent(jax.random.fold_in(streams_of[8], 71), 0),
        "master_weights": draw_master_weights(jax.random.fold_in(streams_of[8], 71), 0),
        "first_moment": draw_first_moment(jax.random.fold_in(streams_of[8], 71), 0),
        "second_moment": jnp.clip(jnp.exp(math.log(4.0) - 2.7725887 * jax.random.uniform(streams_of[4], (D, D), jnp.float32) ** levels(streams_of[4], (D, D), ((0, 8), (1, 16)), -0.2, 0.2)), 0.25, 4.0),
        "step_count": jax.random.randint(streams_of[5], (1,), 1, 24).astype(jnp.int32),
        "language_ids": jax.random.randint(streams_of[6], (1,), 0, LANGS).astype(jnp.int32),
        "language_rates": jnp.clip(jnp.exp(jax.random.uniform(streams_of[7], (LANGS,), jnp.float32, math.log(0.25), math.log(2.0))), 0.25, 2.0),
    }


beta_one = 0.9
beta_two = 0.999
epsilon = 1e-06
decay_weight = 0.1
base_rate = 0.25

def reference(activations, cotangent, master_weights, first_moment, second_moment, step_count, language_ids, language_rates):
    gradient = lax.dot_general(activations, cotangent, (((0,), (0,)), ((), ())), preferred_element_type=jnp.float32)
    steps_done = step_count[0].astype(jnp.float32)
    corr_one = 1.0 - jnp.power(jnp.float32(beta_one), steps_done)
    corr_two = 1.0 - jnp.power(jnp.float32(beta_two), steps_done)
    new_first = beta_one * first_moment + (1.0 - beta_one) * gradient
    new_second = beta_two * second_moment + (1.0 - beta_two) * gradient * gradient
    update = new_first / corr_one / (jnp.sqrt(new_second / corr_two) + epsilon) + decay_weight * master_weights
    weight_sq = jnp.sum(master_weights * master_weights)
    update_sq = jnp.sum(update * update)
    trust = jnp.sqrt(weight_sq) / jnp.sqrt(update_sq)
    picked = jnp.arange(language_rates.shape[0], dtype=jnp.int32) == language_ids[0]
    rate = base_rate * jnp.sum(jnp.where(picked, language_rates, jnp.float32(0.0)))
    new_master = master_weights - rate * trust * update
    new_weights = new_master.astype(jnp.bfloat16)
    return (new_master, new_first, new_second, new_weights)
```

```python
import jax
import jax.numpy as jnp
from jax import lax
from jax.experimental import pallas as pl
from jax.experimental.pallas import tpu as pltpu
from jax.sharding import PartitionSpec as P

beta_one = 0.9
beta_two = 0.999
epsilon = 1e-06
decay_weight = 0.1
base_rate = 0.25

ROWS = 640
COLS = 320
BLOCK = 128
GROUP = 2 * ROWS


def moved(array, dz=0, dc=0, dx=0, dy=0):
    pairs = []
    for z in range(4):
        for c in range(2):
            for x in range(4):
                for y in range(4):
                    src = (2 * z + c) * 16 + 4 * x + y
                    dst = (2 * ((z + dz) % 4) + (c + dc) % 2) * 16 + 4 * ((x + dx) % 4) + (y + dy) % 4
                    pairs.append((src, dst))
    return lax.ppermute(array, ("dp", "mp"), pairs)


def place():
    d = lax.axis_index("dp")
    m = lax.axis_index("mp")
    return d // 2, d % 2, m // 4, m % 4


def prepare_kernel(act, cot, a0, a1, a2, a3, c0, c1, c2, c3):
    z, c, x, y = place()
    for kz, out in enumerate((a0, a1, a2, a3)):
        first = lax.rem(z + kz, 4) * GROUP
        mine = pl.multiple_of(first + c * ROWS, 128)
        other = pl.multiple_of(first + (1 - c) * ROWS, 128)
        out[:, :ROWS] = act[:, pl.ds(mine, ROWS)]
        out[:, ROWS:] = act[:, pl.ds(other, ROWS)]
    for ky, out in enumerate((c0, c1, c2, c3)):
        for dx in range(4):
            start = (4 * lax.rem(x + dx, 4) + lax.rem(y + ky, 4)) * BLOCK
            out[:, dx * BLOCK : (dx + 1) * BLOCK] = cot[:, pl.ds(pl.multiple_of(start, 128), BLOCK)]


def prepare(activations, cotangent_t):
    bf16 = jnp.bfloat16
    return pl.pallas_call(
        prepare_kernel,
        out_shape=[jax.ShapeDtypeStruct((BLOCK, GROUP), bf16)] * 4
        + [jax.ShapeDtypeStruct((COLS, 4 * BLOCK), bf16)] * 4,
        compiler_params=pltpu.CompilerParams(vmem_limit_bytes=32 * 2**20),
        name="prepare",
    )(activations, cotangent_t)


def product_kernel(*refs):
    x0, xp, xm, xd0, xd1, z0, zp, zm, zd0, zd1 = refs[:10]
    outs = refs[10:18]
    a_all, c_all, stage, in_sems, out_sems = refs[18:]
    copies = []
    for kz in range(4):
        for dx, block in ((0, x0), (1, xp), (2, None), (3, xm)):
            if block is None:
                src = (xd0 if kz < 2 else xd1).at[pl.ds((kz % 2) * BLOCK, BLOCK)]
            else:
                src = block.at[pl.ds(kz * BLOCK, BLOCK)]
            copies.append((src, a_all.at[pl.ds((4 * kz + dx) * BLOCK, BLOCK)]))
    width = 4 * BLOCK
    for kz, block in ((0, z0), (1, zm), (3, zp)):
        copies.append((block, c_all.at[:, pl.ds(kz * width, width)]))
    copies.append((zd0, c_all.at[pl.ds(0, 2 * COLS), pl.ds(2 * width, width)]))
    copies.append((zd1, c_all.at[pl.ds(2 * COLS, 2 * COLS), pl.ds(2 * width, width)]))
    started = []
    for k, (src, dst) in enumerate(copies):
        copy = pltpu.make_async_copy(src, dst, in_sems.at[k])
        copy.start()
        started.append(copy)
    for copy in started:
        copy.wait()
    writes = []
    for step, ky in enumerate((2, 1, 3, 0)):
        total = jnp.dot(
            c_all[ky * COLS : (ky + 1) * COLS, :], a_all[...], preferred_element_type=jnp.float32
        )
        for half in (1, 0):
            stage[2 * step + half] = total[:, half * ROWS : (half + 1) * ROWS]
            write = pltpu.make_async_copy(
                stage.at[2 * step + half], outs[2 * ky + half], out_sems.at[2 * step + half]
            )
            write.start()
            writes.append(write)
    for write in writes:
        write.wait()


def product(pieces):
    any_space = pl.BlockSpec(memory_space=pl.ANY)
    return pl.pallas_call(
        product_kernel,
        out_shape=[jax.ShapeDtypeStruct((COLS, ROWS), jnp.float32)] * 8,
        in_specs=[any_space] * 10,
        out_specs=[any_space] * 8,
        scratch_shapes=[
            pltpu.VMEM((16 * BLOCK, GROUP), jnp.bfloat16),
            pltpu.VMEM((4 * COLS, 16 * BLOCK), jnp.bfloat16),
            pltpu.VMEM((8, COLS, ROWS), jnp.float32),
            pltpu.SemaphoreType.DMA((21,)),
            pltpu.SemaphoreType.DMA((8,)),
        ],
        compiler_params=pltpu.CompilerParams(vmem_limit_bytes=40 * 2**20),
        name="product",
    )(*pieces)


def ring_gather(block, axis):
    half = block.shape[0] // 2
    plus = moved(block, **{axis: -1})
    minus = moved(block, **{axis: 1})
    far_first = moved(plus[:half], **{axis: -1})
    far_second = moved(minus[half:], **{axis: 1})
    return [block, plus, minus, far_first, far_second]


def gradient_t(activations, cotangent):
    parts = prepare(activations, cotangent.T)
    acts, cots = parts[:4], parts[4:]
    a_block = jnp.concatenate([acts[0]] + [moved(acts[k], dz=k) for k in (1, 2, 3)], axis=0)
    c_block = jnp.concatenate([cots[0]] + [moved(cots[k], dy=k) for k in (1, 2, 3)], axis=0)
    outs = product(ring_gather(a_block, "dx") + ring_gather(c_block, "dz"))
    sums = {}
    for ky in (2, 1, 3, 0):
        sums[ky] = outs[2 * ky] + moved(outs[2 * ky + 1], dc=1)
    return sums[0] + moved(sums[1], dy=-1) + moved(sums[2], dy=-2) + moved(sums[3], dy=-3)


def total_over_devices(values):
    values = values + moved(values, dc=1)
    for axis in ("dx", "dy", "dz"):
        values = values + moved(values, **{axis: 1}) + moved(values, **{axis: 2}) + moved(values, **{axis: 3})
    return values


def on_device(
    activations,
    cotangent,
    master_weights,
    first_moment,
    second_moment,
    step_count,
    language_ids,
    language_rates,
):
    gradient = gradient_t(activations, cotangent).T
    steps_done = step_count[0].astype(jnp.float32)
    corr_one = 1.0 - jnp.power(jnp.float32(beta_one), steps_done)
    corr_two = 1.0 - jnp.power(jnp.float32(beta_two), steps_done)
    new_first = beta_one * first_moment + (1.0 - beta_one) * gradient
    new_second = beta_two * second_moment + (1.0 - beta_two) * gradient * gradient
    update = (
        new_first / corr_one / (jnp.sqrt(new_second / corr_two) + epsilon)
        + decay_weight * master_weights
    )
    sums = total_over_devices(
        jnp.stack([jnp.sum(master_weights * master_weights), jnp.sum(update * update)])
    )
    trust = jnp.sqrt(sums[0]) / jnp.sqrt(sums[1])
    picked = jnp.arange(language_rates.shape[0], dtype=jnp.int32) == language_ids[0]
    rate = base_rate * jnp.sum(jnp.where(picked, language_rates, jnp.float32(0.0)))
    new_master = master_weights - rate * trust * update
    new_weights = lax.all_gather(new_master.astype(jnp.bfloat16), "dp", axis=0, tiled=True)
    return (new_master, new_first, new_second, new_weights)


def solution(mesh):
    return jax.shard_map(
        on_device,
        mesh=mesh,
        in_specs=(
            P(("dp", "mp"), None),
            P("dp", "mp"),
            P("dp", "mp"),
            P("dp", "mp"),
            P("dp", "mp"),
            P(),
            P(),
            P(),
        ),
        out_specs=(P("dp", "mp"), P("dp", "mp"), P("dp", "mp"), P(None, "mp")),
        check_vma=False,
    )
```

```python
import jax
import jax.numpy as jnp
from jax import lax
from jax.experimental import pallas as pl
from jax.experimental.pallas import tpu as pltpu
from jax.sharding import PartitionSpec as P

beta_one = 0.9
beta_two = 0.999
epsilon = 1e-06
decay_weight = 0.1
base_rate = 0.25

ROWS = 640
COLS = 320
BLOCK = 128
GROUP = 2 * ROWS


def moved(array, dz=0, dc=0, dx=0, dy=0):
    pairs = []
    for z in range(4):
        for c in range(2):
            for x in range(4):
                for y in range(4):
                    src = (2 * z + c) * 16 + 4 * x + y
                    dst = (2 * ((z + dz) % 4) + (c + dc) % 2) * 16 + 4 * ((x + dx) % 4) + (y + dy) % 4
                    pairs.append((src, dst))
    return lax.ppermute(array, ("dp", "mp"), pairs)


def place():
    d = lax.axis_index("dp")
    m = lax.axis_index("mp")
    return d // 2, d % 2, m // 4, m % 4


def prepare_kernel(act, cot, a0, a1, a2, a3, c0, c1, c2, c3, sems):
    z, c, x, y = place()
    copies = []
    for kz, out in enumerate((a0, a1, a2, a3)):
        first = lax.rem(z + kz, 4) * GROUP
        for half, core in enumerate((c, 1 - c)):
            start = pl.multiple_of(first + core * ROWS, 128)
            copies.append((act.at[:, pl.ds(start, ROWS)], out.at[:, pl.ds(half * ROWS, ROWS)]))
    for ky, out in enumerate((c0, c1, c2, c3)):
        for dx in range(4):
            start = (4 * lax.rem(x + dx, 4) + lax.rem(y + ky, 4)) * BLOCK
            start = pl.multiple_of(start, 128)
            copies.append((cot.at[:, pl.ds(start, BLOCK)], out.at[:, pl.ds(dx * BLOCK, BLOCK)]))
    started = [pltpu.make_async_copy(src, dst, sems.at[k]) for k, (src, dst) in enumerate(copies)]
    for copy in started:
        copy.start()
    for copy in started:
        copy.wait()


ANY = pl.BlockSpec(memory_space=pl.ANY)
VMEM = pl.BlockSpec(memory_space=pltpu.VMEM)
SMEM = pl.BlockSpec(memory_space=pltpu.SMEM)


def params(mib):
    return pltpu.CompilerParams(vmem_limit_bytes=mib * 2**20)


def prepare(activations, cotangent_t):
    bf16 = jnp.bfloat16
    return pl.pallas_call(
        prepare_kernel,
        out_shape=[jax.ShapeDtypeStruct((BLOCK, GROUP), bf16)] * 4
        + [jax.ShapeDtypeStruct((COLS, 4 * BLOCK), bf16)] * 4,
        in_specs=[pl.BlockSpec(memory_space=pltpu.HBM)] * 2,
        out_specs=[VMEM] * 8,
        scratch_shapes=[pltpu.SemaphoreType.DMA((24,))],
        compiler_params=params(4),
        name="prepare",
    )(activations, cotangent_t)


def dot(a, b):
    return jnp.dot(a, b, preferred_element_type=jnp.float32)


def near_kernel(x0, xp, xm, z0, zp, zm, *outs):
    acts = jnp.concatenate(
        [x[kz * BLOCK : (kz + 1) * BLOCK, :] for kz in (0, 1, 3) for x in (x0, xp, xm)], axis=0
    )
    for ky, out in enumerate(outs):
        rows = slice(ky * COLS, (ky + 1) * COLS)
        parts = []
        for z in (z0, zm, zp):
            parts += [z[rows, : 2 * BLOCK], z[rows, 3 * BLOCK :]]
        out[...] = dot(jnp.concatenate(parts, axis=1), acts)


def near_product(x0, xp, xm, z0, zp, zm):
    return pl.pallas_call(
        near_kernel,
        out_shape=[jax.ShapeDtypeStruct((COLS, GROUP), jnp.float32)] * 4,
        in_specs=[VMEM] * 6,
        out_specs=[VMEM] * 4,
        compiler_params=params(14),
        name="near_product",
    )(x0, xp, xm, z0, zp, zm)


def far_kernel(*refs):
    x0, xp, xm, xd0, xd1, z0, zp, zm, zd0, zd1 = refs[:10]
    totals = refs[10:14]
    outs = refs[14:]
    acts = jnp.concatenate(
        [x[2 * BLOCK : 3 * BLOCK, :] for x in (x0, xp)]
        + [xd1[:BLOCK, :]]
        + [xm[2 * BLOCK : 3 * BLOCK, :]]
        + [xd0[:BLOCK, :], xd0[BLOCK:, :], xd1[BLOCK:, :]],
        axis=0,
    )
    middle = slice(2 * BLOCK, 3 * BLOCK)
    for ky in (2, 1, 3, 0):
        rows = slice(ky * COLS, (ky + 1) * COLS)
        far = zd0 if ky < 2 else zd1
        parts = [far[(ky % 2) * COLS : (ky % 2 + 1) * COLS, :]]
        parts += [z[rows, middle] for z in (z0, zm, zp)]
        total = totals[ky][...] + dot(jnp.concatenate(parts, axis=1), acts)
        outs[2 * ky][...] = total[:, :ROWS]
        outs[2 * ky + 1][...] = total[:, ROWS:]


def far_product(pieces, totals):
    return pl.pallas_call(
        far_kernel,
        out_shape=[jax.ShapeDtypeStruct((COLS, ROWS), jnp.float32)] * 8,
        in_specs=[VMEM] * 14,
        out_specs=[VMEM] * 8,
        compiler_params=params(14),
        name="far_product",
    )(*pieces, *totals)


def ring_gather(block, axis):
    half = block.shape[0] // 2
    plus = moved(block, **{axis: -1})
    minus = moved(block, **{axis: 1})
    far_first = moved(plus[:half], **{axis: -1})
    far_second = moved(minus[half:], **{axis: 1})
    return [block, plus, minus, far_first, far_second]


def gradient_terms(activations, cotangent):
    parts = prepare(activations, cotangent.T)
    acts, cots = parts[:4], parts[4:]
    a_block = jnp.concatenate([acts[0]] + [moved(acts[k], dz=k) for k in (1, 2, 3)], axis=0)
    c_block = jnp.concatenate([cots[0]] + [moved(cots[k], dy=k) for k in (1, 2, 3)], axis=0)
    a_pieces = ring_gather(a_block, "dx")
    c_pieces = ring_gather(c_block, "dz")
    totals = near_product(*a_pieces[:3], *c_pieces[:3])
    outs = far_product(a_pieces + c_pieces, totals)
    sums = {}
    for ky in (2, 1, 3, 0):
        sums[ky] = outs[2 * ky] + moved(outs[2 * ky + 1], dc=1)
    return [sums[0], moved(sums[1], dy=-1), moved(sums[2], dy=-2), moved(sums[3], dy=-3)]


STRIP = 32


def update_kernel(g0, g1, g2, g3, weights, first, second, scale, new_first, new_second, update, sums):
    inv_one, inv_two = scale[0], scale[1]

    def strip(i, carry):
        rows = pl.ds(pl.multiple_of(i * STRIP, STRIP), STRIP)
        g = (g0[rows, :] + g1[rows, :]) + (g2[rows, :] + g3[rows, :])
        w = weights[rows, :]
        m = beta_one * first[rows, :] + (1.0 - beta_one) * g
        v = beta_two * second[rows, :] + (1.0 - beta_two) * g * g
        u = m * inv_one / (jnp.sqrt(v * inv_two) + epsilon) + decay_weight * w
        new_first[rows, :] = m
        new_second[rows, :] = v
        update[rows, :] = u
        out = []
        for total, term in zip(carry, (w * w, u * u)):
            part = term[:8]
            for k in range(8, STRIP, 8):
                part = part + term[k : k + 8]
            out.append(total + part)
        return tuple(out)

    zero = jnp.zeros((8, ROWS), jnp.float32)
    for k, total in enumerate(lax.fori_loop(0, COLS // STRIP, strip, (zero, zero))):
        part = total[:, :128]
        for j in range(128, ROWS, 128):
            part = part + total[:, j : j + 128]
        sums[8 * k : 8 * k + 8, :] = part


def updated(terms, weights, first, second, scale):
    block = jax.ShapeDtypeStruct((COLS, ROWS), jnp.float32)
    return pl.pallas_call(
        update_kernel,
        out_shape=[block] * 3 + [jax.ShapeDtypeStruct((16, 128), jnp.float32)],
        in_specs=[VMEM] * 7 + [SMEM],
        out_specs=[VMEM] * 4,
        compiler_params=params(6),
        name="update",
    )(*terms, weights, first, second, scale)


def total_over_devices(values):
    values = values + moved(values, dc=1)
    for axis in ("dx", "dy", "dz"):
        values = values + moved(values, **{axis: 1}) + moved(values, **{axis: 2}) + moved(values, **{axis: 3})
    return values


def step_kernel(weights, update, sums, rate, new_master, new_weights):
    weight_sq = jnp.sum(jnp.sum(sums[:8, :], axis=0, keepdims=True), axis=1, keepdims=True)
    update_sq = jnp.sum(jnp.sum(sums[8:, :], axis=0, keepdims=True), axis=1, keepdims=True)
    scale = rate[0] * (jnp.sqrt(weight_sq) / jnp.sqrt(update_sq))

    def strip(i, carry):
        rows = pl.ds(pl.multiple_of(i * STRIP, STRIP), STRIP)
        w = weights[rows, :] - scale * update[rows, :]
        new_master[rows, :] = w
        new_weights[rows, :] = w.astype(jnp.bfloat16)
        return carry

    lax.fori_loop(0, COLS // STRIP, strip, 0)


def stepped(weights, update, sums, rate):
    return pl.pallas_call(
        step_kernel,
        out_shape=[
            jax.ShapeDtypeStruct((COLS, ROWS), jnp.float32),
            jax.ShapeDtypeStruct((COLS, ROWS), jnp.bfloat16),
        ],
        in_specs=[VMEM] * 3 + [SMEM],
        out_specs=[VMEM] * 2,
        compiler_params=params(6),
        name="step",
    )(weights, update, sums, rate)


def assemble_kernel(*refs):
    pieces, out, sems = refs[:8], refs[8], refs[9]
    z, c, x, y = place()
    copies = []
    for k in range(4):
        for half, core in enumerate((c, 1 - c)):
            start = pl.multiple_of((2 * lax.rem(z + k, 4) + core) * ROWS, 128)
            copies.append(
                pltpu.make_async_copy(
                    pieces[2 * k + half], out.at[:, pl.ds(start, ROWS)], sems.at[2 * k + half]
                )
            )
    for copy in copies:
        copy.start()
    for copy in copies:
        copy.wait()


def gathered_rows(block):
    pieces = []
    for k in range(4):
        mine = moved(block, dz=-k) if k else block
        pieces += [mine, moved(mine, dc=1)]
    return pl.pallas_call(
        assemble_kernel,
        out_shape=jax.ShapeDtypeStruct((COLS, 8 * ROWS), block.dtype),
        in_specs=[VMEM] * 8,
        out_specs=ANY,
        scratch_shapes=[pltpu.SemaphoreType.DMA((8,))],
        compiler_params=params(4),
        name="assemble",
    )(*pieces)


def on_device(
    activations,
    cotangent,
    master_weights,
    first_moment,
    second_moment,
    step_count,
    language_ids,
    language_rates,
):
    steps_done = step_count.astype(jnp.float32)
    corr_one = 1.0 - jnp.power(jnp.float32(beta_one), steps_done)
    corr_two = 1.0 - jnp.power(jnp.float32(beta_two), steps_done)
    scale = jnp.concatenate([1.0 / corr_one, 1.0 / corr_two])
    picked = jnp.arange(language_rates.shape[0], dtype=jnp.int32) == language_ids[0]
    rate = base_rate * jnp.sum(jnp.where(picked, language_rates, jnp.float32(0.0)))
    weights = master_weights.T
    terms = gradient_terms(activations, cotangent)
    new_first, new_second, update, sums = updated(
        terms, weights, first_moment.T, second_moment.T, scale
    )
    new_master, mine = stepped(weights, update, total_over_devices(sums), rate.reshape(1))
    return (new_master.T, new_first.T, new_second.T, gathered_rows(mine).T)


def solution(mesh):
    return jax.shard_map(
        on_device,
        mesh=mesh,
        in_specs=(
            P(("dp", "mp"), None),
            P("dp", "mp"),
            P("dp", "mp"),
            P("dp", "mp"),
            P("dp", "mp"),
            P(),
            P(),
            P(),
        ),
        out_specs=(P("dp", "mp"), P("dp", "mp"), P("dp", "mp"), P(None, "mp")),
        check_vma=False,
    )
```

```python
import jax
import jax.numpy as jnp
from jax import lax
from jax.experimental import pallas as pl
from jax.experimental.pallas import tpu as pltpu
from jax.sharding import PartitionSpec as P

beta_one = 0.9
beta_two = 0.999
epsilon = 1e-06
decay_weight = 0.1
base_rate = 0.25

ROWS = 640
COLS = 320
BLOCK = 128
GROUP = 2 * ROWS


def moved(array, dz=0, dc=0, dx=0, dy=0):
    pairs = []
    for z in range(4):
        for c in range(2):
            for x in range(4):
                for y in range(4):
                    src = (2 * z + c) * 16 + 4 * x + y
                    dst = (2 * ((z + dz) % 4) + (c + dc) % 2) * 16 + 4 * ((x + dx) % 4) + (y + dy) % 4
                    pairs.append((src, dst))
    return lax.ppermute(array, ("dp", "mp"), pairs)


def place():
    d = lax.axis_index("dp")
    m = lax.axis_index("mp")
    return d // 2, d % 2, m // 4, m % 4


HBM = pl.BlockSpec(memory_space=pltpu.HBM)
ANY = pl.BlockSpec(memory_space=pl.ANY)
VMEM = pl.BlockSpec(memory_space=pltpu.VMEM)
SMEM = pl.BlockSpec(memory_space=pltpu.SMEM)


def params(mib):
    return pltpu.CompilerParams(vmem_limit_bytes=mib * 2**20)


def copy_all(copies, sems):
    started = [pltpu.make_async_copy(src, dst, sems.at[k]) for k, (src, dst) in enumerate(copies)]
    for copy in started:
        copy.start()
    for copy in started:
        copy.wait()


def rows_kernel(act, *refs):
    outs, sems = refs[:4], refs[4]
    z, c, x, y = place()
    copies = []
    for kz, out in enumerate(outs):
        first = lax.rem(z + kz, 4) * GROUP
        for half, core in enumerate((c, 1 - c)):
            start = pl.multiple_of(first + core * ROWS, 128)
            copies.append((act.at[:, pl.ds(start, ROWS)], out.at[:, pl.ds(half * ROWS, ROWS)]))
    copy_all(copies, sems)


def tokens_kernel(cot, first, *refs):
    outs, sems = refs[:4], refs[4]
    z, c, x, y = place()
    copies = []
    for ky, out in enumerate(outs):
        for dx in range(4):
            start = (4 * lax.rem(x + dx, 4) + lax.rem(y + ky, 4)) * BLOCK
            start = pl.multiple_of(start, 128)
            copies.append((cot.at[:, pl.ds(start, BLOCK)], out.at[:, pl.ds(dx * BLOCK, BLOCK)]))
    copy_all(copies, sems)


def rows_by_z(activations):
    return pl.pallas_call(
        rows_kernel,
        out_shape=[jax.ShapeDtypeStruct((BLOCK, GROUP), jnp.bfloat16)] * 4,
        in_specs=[HBM],
        out_specs=[VMEM] * 4,
        scratch_shapes=[pltpu.SemaphoreType.DMA((8,))],
        compiler_params=params(4),
        name="rows_by_z",
    )(pltpu.with_memory_space_constraint(activations, pltpu.HBM))


def tokens_by_y(cotangent_t, first):
    return pl.pallas_call(
        tokens_kernel,
        out_shape=[jax.ShapeDtypeStruct((COLS, 4 * BLOCK), jnp.bfloat16)] * 4,
        in_specs=[HBM, ANY],
        out_specs=[VMEM] * 4,
        scratch_shapes=[pltpu.SemaphoreType.DMA((16,))],
        compiler_params=params(4),
        name="tokens_by_y",
    )(pltpu.with_memory_space_constraint(cotangent_t, pltpu.HBM), first)


def dot(a, b):
    return jnp.dot(a, b, preferred_element_type=jnp.float32)


def near_kernel(x0, xp, xm, z0, zp, zm, *outs):
    acts = jnp.concatenate(
        [x[kz * BLOCK : (kz + 1) * BLOCK, :] for kz in (0, 1, 3) for x in (x0, xp, xm)], axis=0
    )
    for ky, out in enumerate(outs):
        rows = slice(ky * COLS, (ky + 1) * COLS)
        parts = []
        for z in (z0, zm, zp):
            parts += [z[rows, : 2 * BLOCK], z[rows, 3 * BLOCK :]]
        out[...] = dot(jnp.concatenate(parts, axis=1), acts)


def near_product(x0, xp, xm, z0, zp, zm):
    return pl.pallas_call(
        near_kernel,
        out_shape=[jax.ShapeDtypeStruct((COLS, GROUP), jnp.float32)] * 4,
        in_specs=[VMEM] * 6,
        out_specs=[VMEM] * 4,
        compiler_params=params(14),
        name="near_product",
    )(x0, xp, xm, z0, zp, zm)


def far_kernel(*refs):
    x0, xp, xm, xd0, xd1, z0, zp, zm, zd0, zd1 = refs[:10]
    totals, weights = refs[10:14], refs[14]
    outs, late_weights, sem = refs[15:23], refs[23], refs[24]
    keep = pltpu.make_async_copy(weights, late_weights, sem)
    keep.start()
    acts = jnp.concatenate(
        [x[2 * BLOCK : 3 * BLOCK, :] for x in (x0, xp)]
        + [xd1[:BLOCK, :]]
        + [xm[2 * BLOCK : 3 * BLOCK, :]]
        + [xd0[:BLOCK, :], xd0[BLOCK:, :], xd1[BLOCK:, :]],
        axis=0,
    )
    middle = slice(2 * BLOCK, 3 * BLOCK)
    for ky in (2, 1, 3, 0):
        rows = slice(ky * COLS, (ky + 1) * COLS)
        far = zd0 if ky < 2 else zd1
        parts = [far[(ky % 2) * COLS : (ky % 2 + 1) * COLS, :]]
        parts += [z[rows, middle] for z in (z0, zm, zp)]
        total = totals[ky][...] + dot(jnp.concatenate(parts, axis=1), acts)
        outs[2 * ky][...] = total[:, :ROWS]
        outs[2 * ky + 1][...] = total[:, ROWS:]
    keep.wait()


def far_product(pieces, totals, weights):
    return pl.pallas_call(
        far_kernel,
        out_shape=[jax.ShapeDtypeStruct((COLS, ROWS), jnp.float32)] * 9,
        in_specs=[VMEM] * 14 + [HBM],
        out_specs=[VMEM] * 8 + [HBM],
        scratch_shapes=[pltpu.SemaphoreType.DMA],
        compiler_params=params(14),
        name="far_product",
    )(*pieces, *totals, pltpu.with_memory_space_constraint(weights, pltpu.HBM))


def ring_gather(block, axis):
    half = block.shape[0] // 2
    plus = moved(block, **{axis: -1})
    minus = moved(block, **{axis: 1})
    far_first = moved(plus[:half], **{axis: -1})
    far_second = moved(minus[half:], **{axis: 1})
    return [block, plus, minus, far_first, far_second]


def gradient_terms(activations, cotangent, weights):
    acts = rows_by_z(activations)
    cots = tokens_by_y(cotangent.T, acts[0])
    c_block = jnp.concatenate([cots[0]] + [moved(cots[k], dy=k) for k in (1, 2, 3)], axis=0)
    a_block = jnp.concatenate([acts[0]] + [moved(acts[k], dz=k) for k in (1, 2, 3)], axis=0)
    c_pieces = ring_gather(c_block, "dz")
    a_pieces = ring_gather(a_block, "dx")
    totals = near_product(*a_pieces[:3], *c_pieces[:3])
    *outs, weights = far_product(a_pieces + c_pieces, totals, weights)
    mine, theirs = outs[0::2], outs[1::2]
    half = COLS // 2
    far = moved(theirs[2], dc=1)
    low = moved(mine[2][:half] + far[:half], dy=-1)
    high = moved(mine[2][half:] + far[half:], dy=1)
    down = mine[1] + moved(theirs[1], dc=1)
    up = mine[3] + moved(theirs[3], dc=1)
    own = moved(theirs[0], dc=1)
    down = jnp.concatenate([down[:half] + low, down[half:]], axis=0)
    up = jnp.concatenate([up[:half], up[half:] + high], axis=0)
    return [mine[0], own, moved(down, dy=-1), moved(up, dy=1)], weights


STRIP = 32


def update_kernel(g0, g1, g2, g3, weights, first, second, scale, new_first, new_second, update, sums):
    inv_one, inv_two = scale[0], scale[1]

    def strip(i, carry):
        rows = pl.ds(pl.multiple_of(i * STRIP, STRIP), STRIP)
        g = (g0[rows, :] + g1[rows, :]) + (g2[rows, :] + g3[rows, :])
        w = weights[rows, :]
        m = beta_one * first[rows, :] + (1.0 - beta_one) * g
        v = beta_two * second[rows, :] + (1.0 - beta_two) * g * g
        u = m * inv_one / (jnp.sqrt(v * inv_two) + epsilon) + decay_weight * w
        new_first[rows, :] = m
        new_second[rows, :] = v
        update[rows, :] = u
        out = []
        for total, term in zip(carry, (w * w, u * u)):
            part = term[:8]
            for k in range(8, STRIP, 8):
                part = part + term[k : k + 8]
            out.append(total + part)
        return tuple(out)

    zero = jnp.zeros((8, ROWS), jnp.float32)
    for k, total in enumerate(lax.fori_loop(0, COLS // STRIP, strip, (zero, zero))):
        part = total[:, :128]
        for j in range(128, ROWS, 128):
            part = part + total[:, j : j + 128]
        sums[8 * k : 8 * k + 8, :] = part


def updated(terms, weights, first, second, scale):
    block = jax.ShapeDtypeStruct((COLS, ROWS), jnp.float32)
    return pl.pallas_call(
        update_kernel,
        out_shape=[block] * 3 + [jax.ShapeDtypeStruct((16, 128), jnp.float32)],
        in_specs=[VMEM] * 7 + [SMEM],
        out_specs=[VMEM] * 4,
        compiler_params=params(6),
        name="update",
    )(*terms, weights, first, second, scale)


def total_over_devices(values):
    values = values + moved(values, dc=1)
    for axis in ("dx", "dy", "dz"):
        values = values + moved(values, **{axis: 1}) + moved(values, **{axis: 2}) + moved(values, **{axis: 3})
    return values


def step_kernel(*refs):
    weights, sums, rate = refs[:3]
    updates = refs[3:13]
    new_master, new_weights, held, stage, in_sems, sems = refs[13:]
    z, c, x, y = place()
    order = [(dz, core) for core in (c, 1 - c) for dz in (0, 1, 3, 2)]
    loads = []
    for k, (dz, core) in enumerate(order):
        start = pl.multiple_of((2 * lax.rem(z + dz, 4) + core) * ROWS, 128)
        part = (slice(None), pl.ds(start, ROWS))
        loads.append(pltpu.make_async_copy(weights.at[part], held.at[k], in_sems.at[k]))
        loads[-1].start()
    weight_sq = jnp.sum(jnp.sum(sums[:8, :], axis=0, keepdims=True), axis=1, keepdims=True)
    update_sq = jnp.sum(jnp.sum(sums[8:, :], axis=0, keepdims=True), axis=1, keepdims=True)
    scale = rate[0] * (jnp.sqrt(weight_sq) / jnp.sqrt(update_sq))
    half = COLS // 2
    copies = []
    for core, chosen in ((c, updates[:5]), (1 - c, updates[5:])):
        own, plus, minus, low, high = chosen
        plan = [(0, own, 0, COLS), (1, plus, 0, COLS), (3, minus, 0, COLS), (2, low, 0, half), (2, high, half, half)]
        for dz, update, first, count in plan:
            start = pl.multiple_of((2 * lax.rem(z + dz, 4) + core) * ROWS, 128)
            slot = len(copies)
            load = 4 * (slot // 5) + min(slot % 5, 3)
            if slot % 5 != 4:
                loads[load].wait()

            def strip(i, carry):
                at = pl.multiple_of(i * STRIP, STRIP)
                rows = pl.ds(first + at, STRIP)
                w = held[load, rows, :] - scale * update[pl.ds(at, STRIP), :]
                if slot == 0:
                    new_master[rows, :] = w
                stage[rows, pl.ds(start, ROWS)] = w.astype(jnp.bfloat16)
                return carry

            lax.fori_loop(0, count // STRIP, strip, 0)
            part = (pl.ds(first, count), pl.ds(start, ROWS))
            copy = pltpu.make_async_copy(stage.at[part], new_weights.at[part], sems.at[slot])
            copy.start()
            copies.append(copy)
    for copy in copies:
        copy.wait()


def stepped(weights, sums, rate, updates):
    return pl.pallas_call(
        step_kernel,
        out_shape=[
            jax.ShapeDtypeStruct((COLS, ROWS), jnp.float32),
            jax.ShapeDtypeStruct((COLS, 8 * ROWS), jnp.bfloat16),
        ],
        in_specs=[HBM, VMEM, SMEM] + [VMEM] * 10,
        out_specs=[VMEM, HBM],
        scratch_shapes=[
            pltpu.VMEM((8, COLS, ROWS), jnp.float32),
            pltpu.VMEM((COLS, 8 * ROWS), jnp.bfloat16),
            pltpu.SemaphoreType.DMA((8,)),
            pltpu.SemaphoreType.DMA((10,)),
        ],
        compiler_params=params(14),
        name="step",
    )(pltpu.with_memory_space_constraint(weights, pltpu.HBM), sums, rate, *updates)


def on_device(
    activations,
    cotangent,
    master_weights,
    first_moment,
    second_moment,
    step_count,
    language_ids,
    language_rates,
):
    steps_done = step_count.astype(jnp.float32)
    corr_one = 1.0 - jnp.power(jnp.float32(beta_one), steps_done)
    corr_two = 1.0 - jnp.power(jnp.float32(beta_two), steps_done)
    scale = jnp.concatenate([1.0 / corr_one, 1.0 / corr_two])
    picked = jnp.arange(language_rates.shape[0], dtype=jnp.int32) == language_ids[0]
    rate = base_rate * jnp.sum(jnp.where(picked, language_rates, jnp.float32(0.0)))
    terms, late_weights = gradient_terms(activations, cotangent, master_weights.T)
    all_weights = lax.all_gather(late_weights.T, "dp", axis=0, tiled=True)
    new_first, new_second, update, sums = updated(
        terms, master_weights.T, first_moment.T, second_moment.T, scale
    )
    updates = ring_gather(update, "dz")
    updates += [moved(piece, dc=1) for piece in updates]
    new_master, new_weights = stepped(
        all_weights.T, total_over_devices(sums), rate.reshape(1), updates
    )
    return (new_master.T, new_first.T, new_second.T, new_weights.T)


def solution(mesh):
    return jax.shard_map(
        on_device,
        mesh=mesh,
        in_specs=(
            P(("dp", "mp"), None),
            P("dp", "mp"),
            P("dp", "mp"),
            P("dp", "mp"),
            P("dp", "mp"),
            P(),
            P(),
            P(),
        ),
        out_specs=(P("dp", "mp"), P("dp", "mp"), P("dp", "mp"), P(None, "mp")),
        check_vma=False,
    )
```

```python
import functools

import jax
import jax.numpy as jnp
from jax import lax
from jax.experimental import pallas as pl
from jax.experimental.pallas import tpu as pltpu
from jax.sharding import PartitionSpec as P

beta_one = 0.9
beta_two = 0.999
epsilon = 1e-06
decay_weight = 0.1
base_rate = 0.25

ROWS = 640
COLS = 320
BLOCK = 128
GROUP = 2 * ROWS


def moved(array, dz=0, dc=0, dx=0, dy=0):
    pairs = []
    for z in range(4):
        for c in range(2):
            for x in range(4):
                for y in range(4):
                    src = (2 * z + c) * 16 + 4 * x + y
                    dst = (2 * ((z + dz) % 4) + (c + dc) % 2) * 16 + 4 * ((x + dx) % 4) + (y + dy) % 4
                    pairs.append((src, dst))
    return lax.ppermute(array, ("dp", "mp"), pairs)


def place():
    d = lax.axis_index("dp")
    m = lax.axis_index("mp")
    return d // 2, d % 2, m // 4, m % 4


HBM = pl.BlockSpec(memory_space=pltpu.HBM)
ANY = pl.BlockSpec(memory_space=pl.ANY)
VMEM = pl.BlockSpec(memory_space=pltpu.VMEM)
SMEM = pl.BlockSpec(memory_space=pltpu.SMEM)


def params(mib):
    return pltpu.CompilerParams(vmem_limit_bytes=mib * 2**20)


def copy_all(copies, sems):
    started = [pltpu.make_async_copy(src, dst, sems.at[k]) for k, (src, dst) in enumerate(copies)]
    for copy in started:
        copy.start()
    for copy in started:
        copy.wait()


def rows_kernel(act, first, *refs):
    outs, sems = refs[:4], refs[4]
    z, c, x, y = place()
    copies = []
    for kz, out in enumerate(outs):
        base = lax.rem(z + kz, 4) * GROUP
        for half, core in enumerate((c, 1 - c)):
            start = pl.multiple_of(base + core * ROWS, 128)
            copies.append((act.at[:, pl.ds(start, ROWS)], out.at[:, pl.ds(half * ROWS, ROWS)]))
    copy_all(copies, sems)


def tokens_kernel(cot, *refs):
    outs, sems = refs[:4], refs[4]
    z, c, x, y = place()
    copies = []
    for ky, out in enumerate(outs):
        for dx in range(4):
            start = (4 * lax.rem(x + dx, 4) + lax.rem(y + ky, 4)) * BLOCK
            start = pl.multiple_of(start, 128)
            copies.append((cot.at[:, pl.ds(start, BLOCK)], out.at[:, pl.ds(dx * BLOCK, BLOCK)]))
    copy_all(copies, sems)


def rows_by_z(activations, first):
    return pl.pallas_call(
        rows_kernel,
        out_shape=[jax.ShapeDtypeStruct((BLOCK, GROUP), jnp.bfloat16)] * 4,
        in_specs=[HBM, ANY],
        out_specs=[VMEM] * 4,
        scratch_shapes=[pltpu.SemaphoreType.DMA((8,))],
        compiler_params=params(4),
        name="rows_by_z",
    )(pltpu.with_memory_space_constraint(activations, pltpu.HBM), first)


def tokens_by_y(cotangent_t):
    return pl.pallas_call(
        tokens_kernel,
        out_shape=[jax.ShapeDtypeStruct((COLS, 4 * BLOCK), jnp.bfloat16)] * 4,
        in_specs=[HBM],
        out_specs=[VMEM] * 4,
        scratch_shapes=[pltpu.SemaphoreType.DMA((16,))],
        compiler_params=params(4),
        name="tokens_by_y",
    )(pltpu.with_memory_space_constraint(cotangent_t, pltpu.HBM))


def dot(a, b):
    return jnp.dot(a, b, preferred_element_type=jnp.float32)


def near_kernel(z0, zp, zm, x0, xp, xm, *outs):
    acts = jnp.concatenate(
        [x[kz * BLOCK : (kz + 1) * BLOCK, :] for kz in (0, 1, 3) for x in (x0, xp, xm)], axis=0
    )
    for ky, out in enumerate(outs):
        rows = slice(ky * COLS, (ky + 1) * COLS)
        parts = []
        for z in (z0, zm, zp):
            parts += [z[rows, : 2 * BLOCK], z[rows, 3 * BLOCK :]]
        out[...] = dot(jnp.concatenate(parts, axis=1), acts)


def near_product(z0, zp, zm, x0, xp, xm):
    return pl.pallas_call(
        near_kernel,
        out_shape=[jax.ShapeDtypeStruct((COLS, GROUP), jnp.float32)] * 4,
        in_specs=[VMEM] * 6,
        out_specs=[VMEM] * 4,
        compiler_params=params(14),
        name="near_product",
    )(z0, zp, zm, x0, xp, xm)


def far_kernel(*refs):
    z0, zp, zm, zd0, zd1, x0, xp, xm, xd0, xd1 = refs[:10]
    totals, weights = refs[10:14], refs[14]
    outs, late_weights = refs[15:23], refs[23]
    late_weights[...] = weights[...]
    acts = jnp.concatenate(
        [x[2 * BLOCK : 3 * BLOCK, :] for x in (x0, xp)]
        + [xd1[:BLOCK, :]]
        + [xm[2 * BLOCK : 3 * BLOCK, :]]
        + [xd0[:BLOCK, :], xd0[BLOCK:, :], xd1[BLOCK:, :]],
        axis=0,
    )
    middle = slice(2 * BLOCK, 3 * BLOCK)
    for ky in (2, 1, 3, 0):
        rows = slice(ky * COLS, (ky + 1) * COLS)
        far = zd0 if ky < 2 else zd1
        parts = [far[(ky % 2) * COLS : (ky % 2 + 1) * COLS, :]]
        parts += [z[rows, middle] for z in (z0, zm, zp)]
        total = totals[ky][...] + dot(jnp.concatenate(parts, axis=1), acts)
        outs[2 * ky][...] = total[:, :ROWS]
        outs[2 * ky + 1][...] = total[:, ROWS:]


def far_product(pieces, totals, weights):
    return pl.pallas_call(
        far_kernel,
        out_shape=[jax.ShapeDtypeStruct((COLS, ROWS), jnp.float32)] * 9,
        in_specs=[VMEM] * 15,
        out_specs=[VMEM] * 9,
        compiler_params=params(14),
        name="far_product",
    )(*pieces, *totals, weights)


def ring_gather(block, axis):
    half = block.shape[0] // 2
    plus = moved(block, **{axis: -1})
    minus = moved(block, **{axis: 1})
    far_first = moved(plus[:half], **{axis: -1})
    far_second = moved(minus[half:], **{axis: 1})
    return [block, plus, minus, far_first, far_second]


def gradient_terms(activations, cotangent, weights):
    cots = tokens_by_y(cotangent.T)
    acts = rows_by_z(activations, cots[0])
    c_block = jnp.concatenate([cots[0]] + [moved(cots[k], dy=k) for k in (1, 2, 3)], axis=0)
    a_block = jnp.concatenate([acts[0]] + [moved(acts[k], dz=k) for k in (1, 2, 3)], axis=0)
    c_pieces = ring_gather(c_block, "dz")
    a_pieces = ring_gather(a_block, "dx")
    totals = near_product(*c_pieces[:3], *a_pieces[:3])
    *outs, weights = far_product(c_pieces + a_pieces, totals, weights)
    near = [moved(weights, dz=-1), moved(weights, dz=1)]
    mine, theirs = outs[0::2], outs[1::2]
    half = COLS // 2
    far = moved(theirs[2], dc=1)
    low = moved(mine[2][:half] + far[:half], dy=-1)
    high = moved(mine[2][half:] + far[half:], dy=1)
    down = mine[1] + moved(theirs[1], dc=1)
    up = mine[3] + moved(theirs[3], dc=1)
    own = moved(theirs[0], dc=1)
    down = jnp.concatenate([down[:half] + low, down[half:]], axis=0)
    up = jnp.concatenate([up[:half], up[half:] + high], axis=0)
    return [mine[0], own, moved(down, dy=-1), moved(up, dy=1)], near


STRIP = 32


def update_kernel(g0, g1, g2, g3, weights, first, second, scale, near0, near1, new_first, new_second, update, sums):
    inv_one, inv_two = scale[0], scale[1]

    def strip(i, carry):
        rows = pl.ds(pl.multiple_of(i * STRIP, STRIP), STRIP)
        g = (g0[rows, :] + g1[rows, :]) + (g2[rows, :] + g3[rows, :])
        w = weights[rows, :]
        m = beta_one * first[rows, :] + (1.0 - beta_one) * g
        v = beta_two * second[rows, :] + (1.0 - beta_two) * g * g
        u = m * inv_one / (jnp.sqrt(v * inv_two) + epsilon) + decay_weight * w
        new_first[rows, :] = m
        new_second[rows, :] = v
        update[rows, :] = u
        out = []
        for total, term in zip(carry, (w * w, u * u)):
            part = term[:8]
            for k in range(8, STRIP, 8):
                part = part + term[k : k + 8]
            out.append(total + part)
        return tuple(out)

    zero = jnp.zeros((8, ROWS), jnp.float32)
    for k, total in enumerate(lax.fori_loop(0, COLS // STRIP, strip, (zero, zero))):
        part = total[:, :128]
        for j in range(128, ROWS, 128):
            part = part + total[:, j : j + 128]
        sums[8 * k : 8 * k + 8, :] = part


def updated(terms, weights, first, second, scale, near):
    block = jax.ShapeDtypeStruct((COLS, ROWS), jnp.float32)
    return pl.pallas_call(
        update_kernel,
        out_shape=[block] * 3 + [jax.ShapeDtypeStruct((16, 128), jnp.float32)],
        in_specs=[VMEM] * 7 + [SMEM] + [ANY] * 2,
        out_specs=[VMEM] * 4,
        compiler_params=params(6),
        name="update",
    )(*terms, weights, first, second, scale, *near)


def total_over_devices(values):
    values = values + moved(values, dc=1)
    for axis in ("dx", "dy", "dz"):
        one, two, three = (moved(values, **{axis: k}) for k in (1, 2, 3))
        values = (values + two) + (one + three)
    return values


def scale_of(sums, rate):
    weight_sq = jnp.sum(jnp.sum(sums[:8, :], axis=0, keepdims=True), axis=1, keepdims=True)
    update_sq = jnp.sum(jnp.sum(sums[8:, :], axis=0, keepdims=True), axis=1, keepdims=True)
    return rate[0] * (jnp.sqrt(weight_sq) / jnp.sqrt(update_sq))


def step_kernel(sums, rate, *refs):
    count = len(refs) // 3
    scale = scale_of(sums, rate)

    def strip(i, carry):
        rows = pl.ds(pl.multiple_of(i * STRIP, STRIP), STRIP)
        for weights, update, out in zip(refs[:count], refs[count : 2 * count], refs[2 * count :]):
            out[rows, :] = weights[rows, :] - scale * update[rows, :]
        return carry

    lax.fori_loop(0, COLS // STRIP, strip, 0)


def own_kernel(sums, rate, weights, update, near0, near1, new_master, new_weights):
    step_kernel(sums, rate, weights, update, new_master)
    new_weights[...] = new_master[...].astype(jnp.bfloat16)


def near_step_kernel(sums, rate, *refs):
    step_kernel(sums, rate, *refs[:4], *refs[6:])
    for out, new in zip(refs[4:6], refs[6:]):
        out[...] = new[...].astype(jnp.bfloat16)


def own_step(sums, rate, weights, update, near):
    return pl.pallas_call(
        own_kernel,
        out_shape=[
            jax.ShapeDtypeStruct((COLS, ROWS), jnp.float32),
            jax.ShapeDtypeStruct((COLS, ROWS), jnp.bfloat16),
        ],
        in_specs=[VMEM, SMEM, VMEM, VMEM] + [ANY] * 2,
        out_specs=[VMEM] * 2,
        compiler_params=params(6),
        name="own_step",
    )(sums, rate, weights, update, *near)


def near_step(sums, rate, weights, updates):
    return pl.pallas_call(
        near_step_kernel,
        out_shape=[jax.ShapeDtypeStruct((COLS, ROWS), jnp.bfloat16)] * 2,
        in_specs=[VMEM, SMEM] + [VMEM] * 4,
        out_specs=[VMEM] * 2,
        scratch_shapes=[pltpu.VMEM((COLS, ROWS), jnp.float32)] * 2,
        compiler_params=params(6),
        name="near_step",
    )(sums, rate, *weights, *updates)


def place_kernel(offsets, *refs):
    pieces, out, sems = refs[: 2 * len(offsets)], refs[-2], refs[-1]
    z, c, x, y = place()
    copies = []
    for k, dz in enumerate(offsets):
        for half, core in enumerate((c, 1 - c)):
            start = pl.multiple_of((2 * lax.rem(z + dz, 4) + core) * ROWS, 128)
            copies.append((pieces[2 * k + half], out.at[:, pl.ds(start, ROWS)]))
    copy_all(copies, sems)


def placed(offsets, pieces, held=None):
    count = len(pieces)
    given = [] if held is None else [held]
    return pl.pallas_call(
        functools.partial(place_kernel, offsets),
        out_shape=jax.ShapeDtypeStruct((COLS, 8 * ROWS), jnp.bfloat16),
        in_specs=[VMEM] * count + [HBM] * len(given),
        out_specs=HBM,
        scratch_shapes=[pltpu.SemaphoreType.DMA((count,))],
        input_output_aliases={count: 0} if given else {},
        compiler_params=params(4),
        name="placed",
    )(*pieces, *given)


def on_device(
    activations,
    cotangent,
    master_weights,
    first_moment,
    second_moment,
    step_count,
    language_ids,
    language_rates,
):
    steps_done = step_count.astype(jnp.float32)
    corr_one = 1.0 - jnp.power(jnp.float32(beta_one), steps_done)
    corr_two = 1.0 - jnp.power(jnp.float32(beta_two), steps_done)
    scale = jnp.concatenate([1.0 / corr_one, 1.0 / corr_two])
    picked = jnp.arange(language_rates.shape[0], dtype=jnp.int32) == language_ids[0]
    rate = base_rate * jnp.sum(jnp.where(picked, language_rates, jnp.float32(0.0)))
    weights = master_weights.T
    rate = rate.reshape(1)
    terms, near_weights = gradient_terms(activations, cotangent, weights)
    new_first, new_second, update, sums = updated(
        terms, weights, first_moment.T, second_moment.T, scale, near_weights
    )
    near_updates = [moved(update, dz=-1), moved(update, dz=1)]
    sums = total_over_devices(sums)
    new_master, own = own_step(sums, rate, weights, update, near_updates)
    far = moved(own, dz=2)
    plus, minus = near_step(sums, rate, near_weights, near_updates)
    pieces = []
    for block in (own, plus, minus):
        pieces += [block, moved(block, dc=1)]
    new_weights = placed((0, 1, 3), pieces)
    new_weights = placed((2,), [far, moved(far, dc=1)], new_weights)
    return (new_master.T, new_first.T, new_second.T, new_weights.T)


def solution(mesh):
    return jax.shard_map(
        on_device,
        mesh=mesh,
        in_specs=(
            P(("dp", "mp"), None),
            P("dp", "mp"),
            P("dp", "mp"),
            P("dp", "mp"),
            P("dp", "mp"),
            P(),
            P(),
            P(),
        ),
        out_specs=(P("dp", "mp"), P("dp", "mp"), P("dp", "mp"), P(None, "mp")),
        check_vma=False,
    )
```

```python
import functools

import jax
import jax.numpy as jnp
from jax import lax
from jax.experimental import pallas as pl
from jax.experimental.pallas import tpu as pltpu
from jax.sharding import PartitionSpec as P

beta_one = 0.9
beta_two = 0.999
epsilon = 1e-06
decay_weight = 0.1
base_rate = 0.25

ROWS = 640
COLS = 320
BLOCK = 128
GROUP = 2 * ROWS


def moved(array, dz=0, dc=0, dx=0, dy=0):
    pairs = []
    for z in range(4):
        for c in range(2):
            for x in range(4):
                for y in range(4):
                    src = (2 * z + c) * 16 + 4 * x + y
                    dst = (2 * ((z + dz) % 4) + (c + dc) % 2) * 16 + 4 * ((x + dx) % 4) + (y + dy) % 4
                    pairs.append((src, dst))
    return lax.ppermute(array, ("dp", "mp"), pairs)


def place():
    d = lax.axis_index("dp")
    m = lax.axis_index("mp")
    return d // 2, d % 2, m // 4, m % 4


HBM = pl.BlockSpec(memory_space=pltpu.HBM)
ANY = pl.BlockSpec(memory_space=pl.ANY)
VMEM = pl.BlockSpec(memory_space=pltpu.VMEM)
SMEM = pl.BlockSpec(memory_space=pltpu.SMEM)


def params(mib):
    return pltpu.CompilerParams(vmem_limit_bytes=mib * 2**20)


def copy_all(copies, sems):
    started = [pltpu.make_async_copy(src, dst, sems.at[k]) for k, (src, dst) in enumerate(copies)]
    for copy in started:
        copy.start()
    for copy in started:
        copy.wait()


def prepare_kernel(act, cot, *refs):
    acts, cots, sems = refs[:4], refs[4:8], refs[8]
    z, c, x, y = place()
    copies = []
    for kz, out in enumerate(acts):
        base = lax.rem(z + kz, 4) * GROUP
        for half, core in enumerate((c, 1 - c)):
            start = pl.multiple_of(base + core * ROWS, 128)
            copies.append((act.at[:, pl.ds(start, ROWS)], out.at[:, pl.ds(half * ROWS, ROWS)]))
    for ky, out in enumerate(cots):
        for dx in range(4):
            start = (4 * lax.rem(x + dx, 4) + lax.rem(y + ky, 4)) * BLOCK
            start = pl.multiple_of(start, 128)
            copies.append((cot.at[:, pl.ds(start, BLOCK)], out.at[:, pl.ds(dx * BLOCK, BLOCK)]))
    copy_all(copies, sems)


def prepare(activations, cotangent_t):
    bf16 = jnp.bfloat16
    return pl.pallas_call(
        prepare_kernel,
        out_shape=[jax.ShapeDtypeStruct((BLOCK, GROUP), bf16)] * 4
        + [jax.ShapeDtypeStruct((COLS, 4 * BLOCK), bf16)] * 4,
        in_specs=[HBM] * 2,
        out_specs=[VMEM] * 8,
        scratch_shapes=[pltpu.SemaphoreType.DMA((24,))],
        compiler_params=params(4),
        name="prepare",
    )(
        pltpu.with_memory_space_constraint(activations, pltpu.HBM),
        pltpu.with_memory_space_constraint(cotangent_t, pltpu.HBM),
    )


def keep_kernel(*refs):
    pass


def kept(arrays):
    count = len(arrays)
    return pl.pallas_call(
        keep_kernel,
        out_shape=[jax.ShapeDtypeStruct(a.shape, a.dtype) for a in arrays],
        in_specs=[ANY] * count,
        out_specs=[ANY] * count,
        input_output_aliases={k: k for k in range(count)},
        compiler_params=params(1),
        name="kept",
    )(*arrays)


def dot(a, b):
    return jnp.dot(a, b, preferred_element_type=jnp.float32)


def near_kernel(z0, zp, zm, x0, xp, xm, *outs):
    acts = jnp.concatenate(
        [x[kz * BLOCK : (kz + 1) * BLOCK, :] for kz in (0, 1, 3) for x in (x0, xp, xm)], axis=0
    )
    for ky, out in enumerate(outs):
        rows = slice(ky * COLS, (ky + 1) * COLS)
        parts = []
        for z in (z0, zm, zp):
            parts += [z[rows, : 2 * BLOCK], z[rows, 3 * BLOCK :]]
        out[...] = dot(jnp.concatenate(parts, axis=1), acts)


def near_product(z0, zp, zm, x0, xp, xm):
    return pl.pallas_call(
        near_kernel,
        out_shape=[jax.ShapeDtypeStruct((COLS, GROUP), jnp.float32)] * 4,
        in_specs=[VMEM] * 6,
        out_specs=[VMEM] * 4,
        compiler_params=params(10),
        name="near_product",
    )(z0, zp, zm, x0, xp, xm)


def far_kernel(*refs):
    z0, zp, zm, zd0, zd1, x0, xp, xm, xd0, xd1 = refs[:10]
    totals, weights = refs[10:14], refs[14]
    outs, late_weights = refs[15:23], refs[23]
    late_weights[...] = weights[...]
    acts = jnp.concatenate(
        [x[2 * BLOCK : 3 * BLOCK, :] for x in (x0, xp)]
        + [xd1[:BLOCK, :]]
        + [xm[2 * BLOCK : 3 * BLOCK, :]]
        + [xd0[:BLOCK, :], xd0[BLOCK:, :], xd1[BLOCK:, :]],
        axis=0,
    )
    middle = slice(2 * BLOCK, 3 * BLOCK)
    for ky in (2, 1, 3, 0):
        rows = slice(ky * COLS, (ky + 1) * COLS)
        far = zd0 if ky < 2 else zd1
        parts = [far[(ky % 2) * COLS : (ky % 2 + 1) * COLS, :]]
        parts += [z[rows, middle] for z in (z0, zm, zp)]
        total = totals[ky][...] + dot(jnp.concatenate(parts, axis=1), acts)
        outs[2 * ky][...] = total[:, :ROWS]
        outs[2 * ky + 1][...] = total[:, ROWS:]


def far_product(pieces, totals, weights):
    return pl.pallas_call(
        far_kernel,
        out_shape=[jax.ShapeDtypeStruct((COLS, ROWS), jnp.float32)] * 9,
        in_specs=[VMEM] * 15,
        out_specs=[VMEM] * 9,
        compiler_params=params(10),
        name="far_product",
    )(*pieces, *totals, weights)


def ring_gather(block, axis):
    half = block.shape[0] // 2
    plus = moved(block, **{axis: -1})
    minus = moved(block, **{axis: 1})
    far_first = moved(plus[:half], **{axis: -1})
    far_second = moved(minus[half:], **{axis: 1})
    return [block, plus, minus, far_first, far_second]


def exchanged(blocks, axis):
    parts = {k: moved(blocks[k], **{axis: k}) for k in (2, 1, 3)}
    return jnp.concatenate([blocks[0], parts[1], parts[2], parts[3]], axis=0)


def gradient_terms(activations, cotangent, weights):
    parts = prepare(activations, cotangent.T)
    c_block = exchanged(parts[4:], "dy")
    a_block = exchanged(kept(parts[:4]), "dz")
    c_pieces = ring_gather(c_block, "dz")
    a_pieces = ring_gather(a_block, "dx")
    totals = near_product(*c_pieces[:3], *a_pieces[:3])
    *outs, weights = far_product(c_pieces + a_pieces, totals, weights)
    near = [moved(weights, dz=-1), moved(weights, dz=1)]
    mine, theirs = outs[0::2], outs[1::2]
    half = COLS // 2
    far = moved(theirs[2], dc=1)
    low = moved(mine[2][:half] + far[:half], dy=-1)
    high = moved(mine[2][half:] + far[half:], dy=1)
    one = moved(theirs[1], dc=1)
    three = moved(theirs[3], dc=1)
    down_high = moved(mine[1][half:] + one[half:], dy=-1)
    up_low = moved(mine[3][:half] + three[:half], dy=1)
    own = moved(theirs[0], dc=1)
    down_low = moved(mine[1][:half] + one[:half] + low, dy=-1)
    up_high = moved(mine[3][half:] + three[half:] + high, dy=1)
    return [mine[0], own, down_low, down_high, up_low, up_high], near


STRIP = 32


def update_kernel(*refs):
    own0, own1, down_low, down_high, up_low, up_high, weights, first, second, scale = refs[:10]
    update, gradient, sums = refs[-3:]
    inv_one, inv_two = scale[0], scale[1]
    half = COLS // 2
    carry = (jnp.zeros((8, ROWS), jnp.float32),) * 2
    for base, down, up in ((0, down_low, up_low), (half, down_high, up_high)):

        def strip(i, carry):
            at = pl.multiple_of(i * STRIP, STRIP)
            part, rows = pl.ds(at, STRIP), pl.ds(base + at, STRIP)
            g = (own0[rows, :] + own1[rows, :]) + (down[part, :] + up[part, :])
            w = weights[rows, :]
            m = beta_one * first[rows, :] + (1.0 - beta_one) * g
            v = beta_two * second[rows, :] + (1.0 - beta_two) * g * g
            u = m * inv_one / (jnp.sqrt(v * inv_two) + epsilon) + decay_weight * w
            update[rows, :] = u
            gradient[rows, :] = g
            out = []
            for total, term in zip(carry, (w * w, u * u)):
                part = term[:8]
                for k in range(8, STRIP, 8):
                    part = part + term[k : k + 8]
                out.append(total + part)
            return tuple(out)

        carry = lax.fori_loop(0, half // STRIP, strip, carry)
    for k, total in enumerate(carry):
        part = total[:, :128]
        for j in range(128, ROWS, 128):
            part = part + total[:, j : j + 128]
        sums[8 * k : 8 * k + 8, :] = part


def updated(terms, weights, first, second, scale, near):
    block = jax.ShapeDtypeStruct((COLS, ROWS), jnp.float32)
    return pl.pallas_call(
        update_kernel,
        out_shape=[block] * 2 + [jax.ShapeDtypeStruct((16, 128), jnp.float32)],
        in_specs=[VMEM] * 9 + [SMEM] + [VMEM] * 2,
        out_specs=[VMEM] * 3,
        compiler_params=params(6),
        name="update",
    )(*terms, weights, first, second, scale, *near)


def in_vmem(array):
    return pltpu.with_memory_space_constraint(array, pltpu.VMEM)


def total_over_devices(values):
    values = values + moved(values, dc=1)
    for axis in ("dx", "dy", "dz"):
        one, two, three = (moved(values, **{axis: k}) for k in (1, 2, 3))
        values = (values + two) + (one + three)
    return values


def scale_of(sums, rate):
    weight_sq = jnp.sum(jnp.sum(sums[:8, :], axis=0, keepdims=True), axis=1, keepdims=True)
    update_sq = jnp.sum(jnp.sum(sums[8:, :], axis=0, keepdims=True), axis=1, keepdims=True)
    return rate[0] * (jnp.sqrt(weight_sq) / jnp.sqrt(update_sq))


def step_kernel(sums, rate, *refs):
    weights, near_weights, updates, outs = refs[0], refs[1:3], refs[3:6], refs[6:9]
    plus_low, minus_high, held, sems = refs[9:]
    half = COLS // 2
    loads = []
    for k, base in ((0, 0), (1, half), (0, half), (1, 0)):
        part = pl.ds(base, half)
        load = pltpu.make_async_copy(near_weights[k].at[part], held.at[k, part], sems.at[len(loads)])
        load.start()
        loads.append(load)
    scale = scale_of(sums, rate)

    def block(w, u, out, base, also):
        def strip(i, carry):
            at = pl.multiple_of(i * STRIP, STRIP)
            part, rows = pl.ds(at, STRIP), pl.ds(base + at, STRIP)
            new = (w[rows, :] - scale * u[rows, :]).astype(jnp.bfloat16)
            out[rows, :] = new
            if also is not None:
                also[part, :] = new
            return carry

        lax.fori_loop(0, half // STRIP, strip, 0)

    for base in (0, half):
        block(weights, updates[0], outs[0], base, None)
    for (k, base, also), load in zip(
        ((0, 0, plus_low), (1, half, minus_high), (0, half, None), (1, 0, None)), loads
    ):
        load.wait()
        block(held.at[k], updates[1 + k], outs[1 + k], base, also)


def stepped(sums, rate, weights, updates):
    full = jax.ShapeDtypeStruct((COLS, ROWS), jnp.bfloat16)
    part = jax.ShapeDtypeStruct((COLS // 2, ROWS), jnp.bfloat16)
    return pl.pallas_call(
        step_kernel,
        out_shape=[full] * 3 + [part] * 2,
        in_specs=[VMEM, SMEM, VMEM, HBM, HBM] + [VMEM] * 3,
        out_specs=[VMEM] * 5,
        scratch_shapes=[
            pltpu.VMEM((2, COLS, ROWS), jnp.float32),
            pltpu.SemaphoreType.DMA((4,)),
        ],
        compiler_params=params(6),
        name="step",
    )(sums, rate, *weights, *updates)


STATE_ROWS = 64


def state_kernel(sums, rate, weights, first, second, update, gradient, step, new_master, new_first, new_second):
    scale = scale_of(sums, rate)
    for at in range(0, STATE_ROWS, STRIP):
        rows = slice(at, at + STRIP)
        g = gradient[rows, :]
        new_master[rows, :] = weights[rows, :] - scale * update[rows, :]
        new_first[rows, :] = beta_one * first[rows, :] + (1.0 - beta_one) * g
        new_second[rows, :] = beta_two * second[rows, :] + (1.0 - beta_two) * g * g


def new_state(sums, rate, weights, first, second, update, gradient, step):
    block = pl.BlockSpec((STATE_ROWS, ROWS), lambda i: (i, 0))
    whole = pl.BlockSpec((16, 128), lambda i: (0, 0))
    held = [pltpu.with_memory_space_constraint(a, pltpu.HBM) for a in (weights, first, second)]
    return pl.pallas_call(
        state_kernel,
        grid=(COLS // STATE_ROWS,),
        out_shape=[jax.ShapeDtypeStruct((COLS, ROWS), jnp.float32)] * 3,
        in_specs=[whole, SMEM] + [block] * 5 + [ANY],
        out_specs=[block] * 3,
        compiler_params=params(6),
        name="new_state",
    )(sums, rate, *held, update, gradient, step)


def place_kernel(plan, *refs):
    pieces, out, sems = refs[: 2 * len(plan)], refs[-2], refs[-1]
    z, c, x, y = place()
    copies = []
    for k, (dz, first, count) in enumerate(plan):
        for half, core in enumerate((c, 1 - c)):
            start = pl.multiple_of((2 * lax.rem(z + dz, 4) + core) * ROWS, 128)
            copies.append((pieces[2 * k + half], out.at[pl.ds(first, count), pl.ds(start, ROWS)]))
    copy_all(copies, sems)


def placed(plan, blocks, held=None):
    pieces = []
    for block in blocks:
        pieces += [block, moved(block, dc=1)]
    count = len(pieces)
    given = [] if held is None else [held]
    return pl.pallas_call(
        functools.partial(place_kernel, plan),
        out_shape=jax.ShapeDtypeStruct((COLS, 8 * ROWS), jnp.bfloat16),
        in_specs=[VMEM] * count + [HBM] * len(given),
        out_specs=HBM,
        scratch_shapes=[pltpu.SemaphoreType.DMA((count,))],
        input_output_aliases={count: 0} if given else {},
        compiler_params=params(4),
        name="placed",
    )(*pieces, *given)


def on_device(
    activations,
    cotangent,
    master_weights,
    first_moment,
    second_moment,
    step_count,
    language_ids,
    language_rates,
):
    steps_done = step_count.astype(jnp.float32)
    corr_one = 1.0 - jnp.power(jnp.float32(beta_one), steps_done)
    corr_two = 1.0 - jnp.power(jnp.float32(beta_two), steps_done)
    scale = jnp.concatenate([1.0 / corr_one, 1.0 / corr_two])
    picked = jnp.arange(language_rates.shape[0], dtype=jnp.int32) == language_ids[0]
    rate = base_rate * jnp.sum(jnp.where(picked, language_rates, jnp.float32(0.0)))
    weights = master_weights.T
    rate = rate.reshape(1)
    terms, near_weights = gradient_terms(activations, cotangent, weights)
    first, second = first_moment.T, second_moment.T
    update, gradient, sums = updated(terms, weights, first, second, scale, near_weights)
    near_updates = [moved(update, dz=-1), moved(update, dz=1)]
    sums = total_over_devices(sums)
    own, plus, minus, plus_low, minus_high = stepped(
        sums,
        rate,
        [weights] + [pltpu.with_memory_space_constraint(w, pltpu.HBM) for w in near_weights],
        [in_vmem(u) for u in [update] + near_updates],
    )
    half = COLS // 2
    far = [moved(plus_low, dz=-1), moved(minus_high, dz=1)]
    new_master, new_first, new_second = new_state(
        sums, rate, weights, first, second, update, gradient, own
    )
    near = placed(((0, 0, COLS), (1, 0, COLS), (3, 0, COLS)), [own, plus, minus])
    near, new_master, *far = lax.optimization_barrier((near, new_master, *far))
    new_weights = placed(((2, 0, half), (2, half, half)), far, near)
    return (new_master.T, new_first.T, new_second.T, new_weights.T)


def solution(mesh):
    return jax.shard_map(
        on_device,
        mesh=mesh,
        in_specs=(
            P(("dp", "mp"), None),
            P("dp", "mp"),
            P("dp", "mp"),
            P("dp", "mp"),
            P("dp", "mp"),
            P(),
            P(),
            P(),
        ),
        out_specs=(P("dp", "mp"), P("dp", "mp"), P("dp", "mp"), P(None, "mp")),
        check_vma=False,
    )
```

```python
import functools

import jax
import jax.numpy as jnp
from jax import lax
from jax.experimental import pallas as pl
from jax.experimental.pallas import tpu as pltpu
from jax.sharding import PartitionSpec as P

beta_one = 0.9
beta_two = 0.999
epsilon = 1e-06
decay_weight = 0.1
base_rate = 0.25

ROWS = 640
COLS = 320
BLOCK = 128
GROUP = 2 * ROWS


def moved(array, dz=0, dc=0, dx=0, dy=0):
    pairs = []
    for z in range(4):
        for c in range(2):
            for x in range(4):
                for y in range(4):
                    src = (2 * z + c) * 16 + 4 * x + y
                    dst = (2 * ((z + dz) % 4) + (c + dc) % 2) * 16 + 4 * ((x + dx) % 4) + (y + dy) % 4
                    pairs.append((src, dst))
    return lax.ppermute(array, ("dp", "mp"), pairs)


def place():
    d = lax.axis_index("dp")
    m = lax.axis_index("mp")
    return d // 2, d % 2, m // 4, m % 4


HBM = pl.BlockSpec(memory_space=pltpu.HBM)
ANY = pl.BlockSpec(memory_space=pl.ANY)
VMEM = pl.BlockSpec(memory_space=pltpu.VMEM)
SMEM = pl.BlockSpec(memory_space=pltpu.SMEM)


def params(mib):
    return pltpu.CompilerParams(vmem_limit_bytes=mib * 2**20)


def copy_all(copies, sems):
    started = [pltpu.make_async_copy(src, dst, sems.at[k]) for k, (src, dst) in enumerate(copies)]
    for copy in started:
        copy.start()
    for copy in started:
        copy.wait()


def prepare_kernel(act, cot, *refs):
    acts, cots, sems = refs[:4], refs[4:8], refs[8]
    z, c, x, y = place()
    copies = []
    for kz, out in enumerate(acts):
        base = lax.rem(z + kz, 4) * GROUP
        for half, core in enumerate((c, 1 - c)):
            start = pl.multiple_of(base + core * ROWS, 128)
            copies.append((act.at[:, pl.ds(start, ROWS)], out.at[:, pl.ds(half * ROWS, ROWS)]))
    for ky, out in enumerate(cots):
        for dx in range(4):
            start = (4 * lax.rem(x + dx, 4) + lax.rem(y + ky, 4)) * BLOCK
            start = pl.multiple_of(start, 128)
            copies.append((cot.at[:, pl.ds(start, BLOCK)], out.at[:, pl.ds(dx * BLOCK, BLOCK)]))
    copy_all(copies, sems)


def prepare(activations, cotangent_t):
    bf16 = jnp.bfloat16
    return pl.pallas_call(
        prepare_kernel,
        out_shape=[jax.ShapeDtypeStruct((BLOCK, GROUP), bf16)] * 4
        + [jax.ShapeDtypeStruct((COLS, 4 * BLOCK), bf16)] * 4,
        in_specs=[HBM] * 2,
        out_specs=[VMEM] * 8,
        scratch_shapes=[pltpu.SemaphoreType.DMA((24,))],
        compiler_params=params(4),
        name="prepare",
    )(
        pltpu.with_memory_space_constraint(activations, pltpu.HBM),
        pltpu.with_memory_space_constraint(cotangent_t, pltpu.HBM),
    )


def keep_kernel(*refs):
    pass


def kept(arrays):
    count = len(arrays)
    return pl.pallas_call(
        keep_kernel,
        out_shape=[jax.ShapeDtypeStruct(a.shape, a.dtype) for a in arrays],
        in_specs=[ANY] * count,
        out_specs=[ANY] * count,
        input_output_aliases={k: k for k in range(count)},
        compiler_params=params(1),
        name="kept",
    )(*arrays)


def dot(a, b):
    return jnp.dot(a, b, preferred_element_type=jnp.float32)


def near_kernel(z0, zp, zm, x0, xp, xm, *outs):
    acts = jnp.concatenate(
        [x[kz * BLOCK : (kz + 1) * BLOCK, :] for kz in (0, 1, 3) for x in (x0, xp, xm)], axis=0
    )
    for ky, out in enumerate(outs):
        rows = slice(ky * COLS, (ky + 1) * COLS)
        parts = []
        for z in (z0, zm, zp):
            parts += [z[rows, : 2 * BLOCK], z[rows, 3 * BLOCK :]]
        out[...] = dot(jnp.concatenate(parts, axis=1), acts)


def near_product(z0, zp, zm, x0, xp, xm):
    return pl.pallas_call(
        near_kernel,
        out_shape=[jax.ShapeDtypeStruct((COLS, GROUP), jnp.float32)] * 4,
        in_specs=[VMEM] * 6,
        out_specs=[VMEM] * 4,
        compiler_params=params(14),
        name="near_product",
    )(z0, zp, zm, x0, xp, xm)


def far_kernel(order, *refs):
    z0, zp, zm, zd0, zd1, x0, xp, xm, xd0, xd1 = refs[:10]
    totals, outs = refs[10 : 10 + len(order)], refs[11 + len(order) : -1]
    refs[-1][...] = refs[10 + len(order)][...]
    acts = jnp.concatenate(
        [x[2 * BLOCK : 3 * BLOCK, :] for x in (x0, xp)]
        + [xd1[:BLOCK, :]]
        + [xm[2 * BLOCK : 3 * BLOCK, :]]
        + [xd0[:BLOCK, :], xd0[BLOCK:, :], xd1[BLOCK:, :]],
        axis=0,
    )
    middle = slice(2 * BLOCK, 3 * BLOCK)
    for k, ky in enumerate(order):
        rows = slice(ky * COLS, (ky + 1) * COLS)
        far = zd0 if ky < 2 else zd1
        parts = [far[(ky % 2) * COLS : (ky % 2 + 1) * COLS, :]]
        parts += [z[rows, middle] for z in (z0, zm, zp)]
        total = totals[k][...] + dot(jnp.concatenate(parts, axis=1), acts)
        outs[2 * k][...] = total[:, :ROWS]
        outs[2 * k + 1][...] = total[:, ROWS:]


def far_product(order, pieces, totals, also):
    outs = pl.pallas_call(
        functools.partial(far_kernel, order),
        out_shape=[jax.ShapeDtypeStruct((COLS, ROWS), jnp.float32)] * (2 * len(order))
        + [jax.ShapeDtypeStruct(also.shape, also.dtype)],
        in_specs=[VMEM] * (11 + len(order)),
        out_specs=[VMEM] * (2 * len(order) + 1),
        compiler_params=params(14),
        name="far_product",
    )(*pieces, *[totals[ky] for ky in order], also)
    return {ky: (outs[2 * k], outs[2 * k + 1]) for k, ky in enumerate(order)}, outs[-1]


def ring_gather(block, axis):
    half = block.shape[0] // 2
    plus = moved(block, **{axis: -1})
    minus = moved(block, **{axis: 1})
    far_first = moved(plus[:half], **{axis: -1})
    far_second = moved(minus[half:], **{axis: 1})
    return [block, plus, minus, far_first, far_second]


def exchanged(blocks, axis):
    parts = {k: moved(blocks[k], **{axis: k}) for k in (2, 1, 3)}
    return jnp.concatenate([blocks[0], parts[1], parts[2], parts[3]], axis=0)


def gradient_terms(activations, cotangent, weights):
    parts = prepare(activations, cotangent.T)
    c_block = exchanged(parts[4:], "dy")
    a_block = exchanged(kept(parts[:4]), "dz")
    c_pieces = ring_gather(c_block, "dz")
    a_pieces = ring_gather(a_block, "dx")
    totals = near_product(*c_pieces[:3], *a_pieces[:3])
    terms, weights = far_product((2,), c_pieces + a_pieces, totals, weights)
    half = COLS // 2
    far = moved(terms[2][1], dc=1)
    others, weights = far_product((1, 3, 0), c_pieces + a_pieces, totals, weights)
    terms |= others
    low = moved(terms[2][0][:half] + far[:half], dy=-1)
    high = moved(terms[2][0][half:] + far[half:], dy=1)
    down = terms[1][0] + moved(terms[1][1], dc=1)
    up = terms[3][0] + moved(terms[3][1], dc=1)
    own = moved(terms[0][1], dc=1)
    near = [moved(weights, dz=-1), moved(weights, dz=1)]
    down = jnp.concatenate([down[:half] + low, down[half:]], axis=0)
    up = jnp.concatenate([up[:half], up[half:] + high], axis=0)
    return [terms[0][0], own, moved(down, dy=-1), moved(up, dy=1)], near


STRIP = 32


def update_kernel(*refs):
    own0, own1, down, up, weights, first, second, scale = refs[:8]
    new_first, new_second, update, sums, held, sems = refs[10:]
    inv_one, inv_two = scale[0], scale[1]
    half = COLS // 2
    carry = (jnp.zeros((8, ROWS), jnp.float32),) * 2
    copies = []
    for base in (0, half):

        def strip(i, carry):
            rows = pl.ds(base + pl.multiple_of(i * STRIP, STRIP), STRIP)
            g = (own0[rows, :] + own1[rows, :]) + (down[rows, :] + up[rows, :])
            w = weights[rows, :]
            m = beta_one * first[rows, :] + (1.0 - beta_one) * g
            v = beta_two * second[rows, :] + (1.0 - beta_two) * g * g
            u = m * inv_one / (jnp.sqrt(v * inv_two) + epsilon) + decay_weight * w
            held[0, rows, :] = m
            held[1, rows, :] = v
            update[rows, :] = u
            out = []
            for total, term in zip(carry, (w * w, u * u)):
                part = term[:8]
                for k in range(8, STRIP, 8):
                    part = part + term[k : k + 8]
                out.append(total + part)
            return tuple(out)

        carry = lax.fori_loop(0, half // STRIP, strip, carry)
        for k, out in enumerate((new_first, new_second)):
            rows = pl.ds(base, half)
            copies.append(pltpu.make_async_copy(held.at[k, rows], out.at[rows], sems.at[len(copies)]))
            copies[-1].start()
    for k, total in enumerate(carry):
        part = total[:, :128]
        for j in range(128, ROWS, 128):
            part = part + total[:, j : j + 128]
        sums[8 * k : 8 * k + 8, :] = part
    for copy in copies:
        copy.wait()


def updated(terms, weights, first, second, scale, near):
    block = jax.ShapeDtypeStruct((COLS, ROWS), jnp.float32)
    return pl.pallas_call(
        update_kernel,
        out_shape=[block] * 3 + [jax.ShapeDtypeStruct((16, 128), jnp.float32)],
        in_specs=[VMEM] * 7 + [SMEM] + [ANY] * 2,
        out_specs=[HBM] * 2 + [VMEM] * 2,
        scratch_shapes=[
            pltpu.VMEM((2, COLS, ROWS), jnp.float32),
            pltpu.SemaphoreType.DMA((4,)),
        ],
        compiler_params=params(6),
        name="update",
    )(*terms, weights, first, second, scale, *near)


def total_over_devices(values):
    values = values + moved(values, dc=1)
    for axis in ("dx", "dy", "dz"):
        one, two, three = (moved(values, **{axis: k}) for k in (1, 2, 3))
        values = (values + two) + (one + three)
    return values


def scale_of(sums, rate):
    weight_sq = jnp.sum(jnp.sum(sums[:8, :], axis=0, keepdims=True), axis=1, keepdims=True)
    update_sq = jnp.sum(jnp.sum(sums[8:, :], axis=0, keepdims=True), axis=1, keepdims=True)
    return rate[0] * (jnp.sqrt(weight_sq) / jnp.sqrt(update_sq))


def step_kernel(sums, rate, weights, update, near0, near1, new_weights):
    scale = scale_of(sums, rate)

    def strip(i, carry):
        rows = pl.ds(pl.multiple_of(i * STRIP, STRIP), STRIP)
        new_weights[rows, :] = (weights[rows, :] - scale * update[rows, :]).astype(jnp.bfloat16)
        return carry

    lax.fori_loop(0, COLS // STRIP, strip, 0)


def own_step(sums, rate, weights, update, near):
    return pl.pallas_call(
        step_kernel,
        out_shape=jax.ShapeDtypeStruct((COLS, ROWS), jnp.bfloat16),
        in_specs=[VMEM, SMEM, VMEM, VMEM] + [ANY] * 2,
        out_specs=VMEM,
        compiler_params=params(6),
        name="own_step",
    )(sums, rate, weights, update, *near)


def near_step_kernel(sums, rate, w, wp, wm, u, up, um, own, new_master, plus, minus):
    scale = scale_of(sums, rate)

    def strip(i, carry):
        rows = pl.ds(pl.multiple_of(i * STRIP, STRIP), STRIP)
        new_master[rows, :] = w[rows, :] - scale * u[rows, :]
        plus[rows, :] = (wp[rows, :] - scale * up[rows, :]).astype(jnp.bfloat16)
        minus[rows, :] = (wm[rows, :] - scale * um[rows, :]).astype(jnp.bfloat16)
        return carry

    lax.fori_loop(0, COLS // STRIP, strip, 0)


def near_step(sums, rate, weights, updates, own):
    return pl.pallas_call(
        near_step_kernel,
        out_shape=[jax.ShapeDtypeStruct((COLS, ROWS), jnp.float32)]
        + [jax.ShapeDtypeStruct((COLS, ROWS), jnp.bfloat16)] * 2,
        in_specs=[VMEM, SMEM] + [VMEM] * 6 + [ANY],
        out_specs=[VMEM] * 3,
        compiler_params=params(6),
        name="near_step",
    )(sums, rate, *weights, *updates, own)


def place_kernel(offsets, *refs):
    pieces, out, sems = refs[: 2 * len(offsets)], refs[-2], refs[-1]
    z, c, x, y = place()
    copies = []
    for k, dz in enumerate(offsets):
        for half, core in enumerate((c, 1 - c)):
            start = pl.multiple_of((2 * lax.rem(z + dz, 4) + core) * ROWS, 128)
            copies.append((pieces[2 * k + half], out.at[:, pl.ds(start, ROWS)]))
    copy_all(copies, sems)


def placed(offsets, pieces, held=None):
    count = len(pieces)
    given = [] if held is None else [held]
    return pl.pallas_call(
        functools.partial(place_kernel, offsets),
        out_shape=jax.ShapeDtypeStruct((COLS, 8 * ROWS), jnp.bfloat16),
        in_specs=[VMEM] * count + [HBM] * len(given),
        out_specs=HBM,
        scratch_shapes=[pltpu.SemaphoreType.DMA((count,))],
        input_output_aliases={count: 0} if given else {},
        compiler_params=params(4),
        name="placed",
    )(*pieces, *given)


def on_device(
    activations,
    cotangent,
    master_weights,
    first_moment,
    second_moment,
    step_count,
    language_ids,
    language_rates,
):
    steps_done = step_count.astype(jnp.float32)
    corr_one = 1.0 - jnp.power(jnp.float32(beta_one), steps_done)
    corr_two = 1.0 - jnp.power(jnp.float32(beta_two), steps_done)
    scale = jnp.concatenate([1.0 / corr_one, 1.0 / corr_two])
    picked = jnp.arange(language_rates.shape[0], dtype=jnp.int32) == language_ids[0]
    rate = base_rate * jnp.sum(jnp.where(picked, language_rates, jnp.float32(0.0)))
    weights = master_weights.T
    rate = rate.reshape(1)
    terms, near_weights = gradient_terms(activations, cotangent, weights)
    new_first, new_second, update, sums = updated(
        terms, weights, first_moment.T, second_moment.T, scale, near_weights
    )
    near_updates = [moved(update, dz=-1), moved(update, dz=1)]
    sums = total_over_devices(sums)
    own = own_step(sums, rate, weights, update, near_updates)
    far = moved(own, dz=2)
    new_master, plus, minus = near_step(
        sums, rate, [weights] + near_weights, [update] + near_updates, own
    )
    pieces = []
    for block in (own, plus, minus):
        pieces += [block, moved(block, dc=1)]
    near = placed((0, 1, 3), pieces)
    new_weights = placed((2,), [far, moved(far, dc=1)], near)
    return (new_master.T, new_first.T, new_second.T, new_weights.T)


def solution(mesh):
    return jax.shard_map(
        on_device,
        mesh=mesh,
        in_specs=(
            P(("dp", "mp"), None),
            P("dp", "mp"),
            P("dp", "mp"),
            P("dp", "mp"),
            P("dp", "mp"),
            P(),
            P(),
            P(),
        ),
        out_specs=(P("dp", "mp"), P("dp", "mp"), P("dp", "mp"), P(None, "mp")),
        check_vma=False,
    )
```

```python
import functools

import jax
import jax.numpy as jnp
from jax import lax
from jax.experimental import pallas as pl
from jax.experimental.pallas import tpu as pltpu
from jax.sharding import PartitionSpec as P

beta_one = 0.9
beta_two = 0.999
epsilon = 1e-06
decay_weight = 0.1
base_rate = 0.25

ROWS = 640
COLS = 320
BLOCK = 128
GROUP = 2 * ROWS


def moved(array, dz=0, dc=0, dx=0, dy=0):
    pairs = []
    for z in range(4):
        for c in range(2):
            for x in range(4):
                for y in range(4):
                    src = (2 * z + c) * 16 + 4 * x + y
                    dst = (2 * ((z + dz) % 4) + (c + dc) % 2) * 16 + 4 * ((x + dx) % 4) + (y + dy) % 4
                    pairs.append((src, dst))
    return lax.ppermute(array, ("dp", "mp"), pairs)


def place():
    d = lax.axis_index("dp")
    m = lax.axis_index("mp")
    return d // 2, d % 2, m // 4, m % 4


HBM = pl.BlockSpec(memory_space=pltpu.HBM)
ANY = pl.BlockSpec(memory_space=pl.ANY)
VMEM = pl.BlockSpec(memory_space=pltpu.VMEM)
SMEM = pl.BlockSpec(memory_space=pltpu.SMEM)


def params(mib):
    return pltpu.CompilerParams(vmem_limit_bytes=mib * 2**20)


def copy_all(copies, sems):
    started = [pltpu.make_async_copy(src, dst, sems.at[k]) for k, (src, dst) in enumerate(copies)]
    for copy in started:
        copy.start()
    for copy in started:
        copy.wait()


def prepare_kernel(act, cot, *refs):
    acts, cots, sems = refs[:4], refs[4:8], refs[8]
    z, c, x, y = place()
    copies = []
    for kz, out in enumerate(acts):
        base = lax.rem(z + kz, 4) * GROUP
        for half, core in enumerate((c, 1 - c)):
            start = pl.multiple_of(base + core * ROWS, 128)
            copies.append((act.at[:, pl.ds(start, ROWS)], out.at[:, pl.ds(half * ROWS, ROWS)]))
    for ky, out in enumerate(cots):
        for dx in range(4):
            start = (4 * lax.rem(x + dx, 4) + lax.rem(y + ky, 4)) * BLOCK
            start = pl.multiple_of(start, 128)
            copies.append((cot.at[:, pl.ds(start, BLOCK)], out.at[:, pl.ds(dx * BLOCK, BLOCK)]))
    copy_all(copies, sems)


def prepare(activations, cotangent_t):
    bf16 = jnp.bfloat16
    return pl.pallas_call(
        prepare_kernel,
        out_shape=[jax.ShapeDtypeStruct((BLOCK, GROUP), bf16)] * 4
        + [jax.ShapeDtypeStruct((COLS, 4 * BLOCK), bf16)] * 4,
        in_specs=[HBM] * 2,
        out_specs=[VMEM] * 8,
        scratch_shapes=[pltpu.SemaphoreType.DMA((24,))],
        compiler_params=params(4),
        name="prepare",
    )(
        pltpu.with_memory_space_constraint(activations, pltpu.HBM),
        pltpu.with_memory_space_constraint(cotangent_t, pltpu.HBM),
    )


def keep_kernel(*refs):
    pass


def kept(arrays):
    count = len(arrays)
    return pl.pallas_call(
        keep_kernel,
        out_shape=[jax.ShapeDtypeStruct(a.shape, a.dtype) for a in arrays],
        in_specs=[ANY] * count,
        out_specs=[ANY] * count,
        input_output_aliases={k: k for k in range(count)},
        compiler_params=params(1),
        name="kept",
    )(*arrays)


def dot(a, b):
    return jnp.dot(a, b, preferred_element_type=jnp.float32)


def near_kernel(z0, zp, zm, x0, xp, xm, *outs):
    acts = jnp.concatenate(
        [x[kz * BLOCK : (kz + 1) * BLOCK, :] for kz in (0, 1, 3) for x in (x0, xp, xm)], axis=0
    )
    for ky, out in enumerate(outs):
        rows = slice(ky * COLS, (ky + 1) * COLS)
        parts = []
        for z in (z0, zm, zp):
            parts += [z[rows, : 2 * BLOCK], z[rows, 3 * BLOCK :]]
        out[...] = dot(jnp.concatenate(parts, axis=1), acts)


def near_product(z0, zp, zm, x0, xp, xm):
    return pl.pallas_call(
        near_kernel,
        out_shape=[jax.ShapeDtypeStruct((COLS, GROUP), jnp.float32)] * 4,
        in_specs=[VMEM] * 6,
        out_specs=[VMEM] * 4,
        compiler_params=params(14),
        name="near_product",
    )(z0, zp, zm, x0, xp, xm)


def middle_kernel(z0, zp, zm, x0, xp, xm, xd0, xd1, *refs):
    del x0, xp, xm
    rhs = jnp.concatenate([xd0[:BLOCK, :], xd0[BLOCK:, :], xd1[BLOCK:, :]], axis=0)
    for ky in range(4):
        rows = slice(ky * COLS, (ky + 1) * COLS)
        parts = [z[rows, 2 * BLOCK : 3 * BLOCK] for z in (z0, zm, zp)]
        refs[4 + ky][...] = refs[ky][...] + dot(jnp.concatenate(parts, axis=1), rhs)


def middle_product(c_near, a_pieces, totals):
    return pl.pallas_call(
        middle_kernel,
        out_shape=[jax.ShapeDtypeStruct((COLS, GROUP), jnp.float32)] * 4,
        in_specs=[VMEM] * 12,
        out_specs=[VMEM] * 4,
        input_output_aliases={8 + k: k for k in range(4)},
        compiler_params=params(14),
        name="middle_product",
    )(*c_near, *a_pieces, *totals)


def far_kernel(order, *refs):
    zd0, zd1, x0, xp, xm, xd0, xd1 = refs[:7]
    count = len(order)
    totals, outs = refs[7 : 7 + count], refs[8 + count : -1]
    refs[-1][...] = refs[7 + count][...]
    last = slice(2 * BLOCK, 3 * BLOCK)
    rhs = jnp.concatenate([x0[last, :], xp[last, :], xd1[:BLOCK, :], xm[last, :]], axis=0)
    for k, ky in enumerate(order):
        far = zd0 if ky < 2 else zd1
        total = totals[k][...] + dot(far[(ky % 2) * COLS : (ky % 2 + 1) * COLS, :], rhs)
        outs[2 * k][...] = total[:, :ROWS]
        outs[2 * k + 1][...] = total[:, ROWS:]


def far_product(order, pieces, totals, also):
    count = len(order)
    outs = pl.pallas_call(
        functools.partial(far_kernel, order),
        out_shape=[jax.ShapeDtypeStruct((COLS, ROWS), jnp.float32)] * (2 * count)
        + [jax.ShapeDtypeStruct(also.shape, also.dtype)],
        in_specs=[VMEM] * (8 + count),
        out_specs=[VMEM] * (2 * count + 1),
        compiler_params=params(14),
        name="far_product",
    )(*pieces, *[totals[ky] for ky in order], also)
    return {ky: (outs[2 * k], outs[2 * k + 1]) for k, ky in enumerate(order)}, outs[-1]


def ring_gather(block, axis):
    half = block.shape[0] // 2
    plus = moved(block, **{axis: -1})
    minus = moved(block, **{axis: 1})
    far_first = moved(plus[:half], **{axis: -1})
    far_second = moved(minus[half:], **{axis: 1})
    return [block, plus, minus, far_first, far_second]


def exchanged(blocks, axis):
    parts = {k: moved(blocks[k], **{axis: k}) for k in (2, 1, 3)}
    return jnp.concatenate([blocks[0], parts[1], parts[2], parts[3]], axis=0)


def gradient_terms(activations, cotangent, weights):
    parts = prepare(activations, cotangent.T)
    c_block = exchanged(parts[4:], "dy")
    a_block = exchanged(kept(parts[:4]), "dz")
    c_pieces = ring_gather(c_block, "dz")
    a_pieces = ring_gather(a_block, "dx")
    totals = near_product(*c_pieces[:3], *a_pieces[:3])
    totals = middle_product(c_pieces[:3], a_pieces, totals)
    far_pieces = c_pieces[3:] + a_pieces
    terms, weights = far_product((2,), far_pieces, totals, weights)
    half = COLS // 2
    far = moved(terms[2][1], dc=1)
    others, weights = far_product((1, 3, 0), far_pieces, totals, weights)
    terms |= others
    low = moved(terms[2][0][:half] + far[:half], dy=-1)
    high = moved(terms[2][0][half:] + far[half:], dy=1)
    down = terms[1][0] + moved(terms[1][1], dc=1)
    up = terms[3][0] + moved(terms[3][1], dc=1)
    own = moved(terms[0][1], dc=1)
    near = [moved(weights, dz=-1), moved(weights, dz=1)]
    down = jnp.concatenate([down[:half] + low, down[half:]], axis=0)
    up = jnp.concatenate([up[:half], up[half:] + high], axis=0)
    return [terms[0][0], own, moved(down, dy=-1), moved(up, dy=1)], near


STRIP = 32


def update_kernel(*refs):
    own0, own1, down, up, weights, first, second, scale = refs[:8]
    new_first, new_second, update, sums, held, sems = refs[10:]
    inv_one, inv_two = scale[0], scale[1]
    half = COLS // 2
    carry = (jnp.zeros((8, ROWS), jnp.float32),) * 2
    copies = []
    for base in (0, half):

        def strip(i, carry):
            rows = pl.ds(base + pl.multiple_of(i * STRIP, STRIP), STRIP)
            g = (own0[rows, :] + own1[rows, :]) + (down[rows, :] + up[rows, :])
            w = weights[rows, :]
            m = beta_one * first[rows, :] + (1.0 - beta_one) * g
            v = beta_two * second[rows, :] + (1.0 - beta_two) * g * g
            u = m * inv_one / (jnp.sqrt(v * inv_two) + epsilon) + decay_weight * w
            held[0, rows, :] = m
            held[1, rows, :] = v
            update[rows, :] = u
            out = []
            for total, term in zip(carry, (w * w, u * u)):
                part = term[:8]
                for k in range(8, STRIP, 8):
                    part = part + term[k : k + 8]
                out.append(total + part)
            return tuple(out)

        carry = lax.fori_loop(0, half // STRIP, strip, carry)
        for k, out in enumerate((new_first, new_second)):
            rows = pl.ds(base, half)
            copies.append(pltpu.make_async_copy(held.at[k, rows], out.at[rows], sems.at[len(copies)]))
            copies[-1].start()
    for k, total in enumerate(carry):
        part = total[:, :128]
        for j in range(128, ROWS, 128):
            part = part + total[:, j : j + 128]
        sums[8 * k : 8 * k + 8, :] = part
    for copy in copies:
        copy.wait()


def updated(terms, weights, first, second, scale, near):
    block = jax.ShapeDtypeStruct((COLS, ROWS), jnp.float32)
    return pl.pallas_call(
        update_kernel,
        out_shape=[block] * 3 + [jax.ShapeDtypeStruct((16, 128), jnp.float32)],
        in_specs=[VMEM] * 7 + [SMEM] + [ANY] * 2,
        out_specs=[HBM] * 2 + [VMEM] * 2,
        scratch_shapes=[
            pltpu.VMEM((2, COLS, ROWS), jnp.float32),
            pltpu.SemaphoreType.DMA((4,)),
        ],
        compiler_params=params(6),
        name="update",
    )(*terms, weights, first, second, scale, *near)


def total_over_devices(values):
    values = values + moved(values, dc=1)
    for axis in ("dx", "dy", "dz"):
        one, two, three = (moved(values, **{axis: k}) for k in (1, 2, 3))
        values = (values + two) + (one + three)
    return values


def scale_of(sums, rate):
    weight_sq = jnp.sum(jnp.sum(sums[:8, :], axis=0, keepdims=True), axis=1, keepdims=True)
    update_sq = jnp.sum(jnp.sum(sums[8:, :], axis=0, keepdims=True), axis=1, keepdims=True)
    return rate[0] * (jnp.sqrt(weight_sq) / jnp.sqrt(update_sq))


def step_kernel(sums, rate, weights, update, near0, near1, new_weights):
    scale = scale_of(sums, rate)

    def strip(i, carry):
        rows = pl.ds(pl.multiple_of(i * STRIP, STRIP), STRIP)
        new_weights[rows, :] = (weights[rows, :] - scale * update[rows, :]).astype(jnp.bfloat16)
        return carry

    lax.fori_loop(0, COLS // STRIP, strip, 0)


def own_step(sums, rate, weights, update, near):
    return pl.pallas_call(
        step_kernel,
        out_shape=jax.ShapeDtypeStruct((COLS, ROWS), jnp.bfloat16),
        in_specs=[VMEM, SMEM, VMEM, VMEM] + [ANY] * 2,
        out_specs=VMEM,
        compiler_params=params(6),
        name="own_step",
    )(sums, rate, weights, update, *near)


def near_step_kernel(sums, rate, w, wp, wm, u, up, um, own, new_master, plus, minus):
    scale = scale_of(sums, rate)

    def strip(i, carry):
        rows = pl.ds(pl.multiple_of(i * STRIP, STRIP), STRIP)
        new_master[rows, :] = w[rows, :] - scale * u[rows, :]
        plus[rows, :] = (wp[rows, :] - scale * up[rows, :]).astype(jnp.bfloat16)
        minus[rows, :] = (wm[rows, :] - scale * um[rows, :]).astype(jnp.bfloat16)
        return carry

    lax.fori_loop(0, COLS // STRIP, strip, 0)


def near_step(sums, rate, weights, updates, own):
    return pl.pallas_call(
        near_step_kernel,
        out_shape=[jax.ShapeDtypeStruct((COLS, ROWS), jnp.float32)]
        + [jax.ShapeDtypeStruct((COLS, ROWS), jnp.bfloat16)] * 2,
        in_specs=[VMEM, SMEM] + [VMEM] * 6 + [ANY],
        out_specs=[VMEM] * 3,
        compiler_params=params(6),
        name="near_step",
    )(sums, rate, *weights, *updates, own)


def place_kernel(offsets, *refs):
    pieces, out, sems = refs[: 2 * len(offsets)], refs[-2], refs[-1]
    z, c, x, y = place()
    copies = []
    for k, dz in enumerate(offsets):
        for half, core in enumerate((c, 1 - c)):
            start = pl.multiple_of((2 * lax.rem(z + dz, 4) + core) * ROWS, 128)
            for first in range(0, COLS, COLS // 2):
                rows = pl.ds(first, COLS // 2)
                copies.append((pieces[2 * k + half].at[rows], out.at[rows, pl.ds(start, ROWS)]))
    copy_all(copies, sems)


def placed(offsets, pieces, held=None):
    count = len(pieces)
    given = [] if held is None else [held]
    return pl.pallas_call(
        functools.partial(place_kernel, offsets),
        out_shape=jax.ShapeDtypeStruct((COLS, 8 * ROWS), jnp.bfloat16),
        in_specs=[VMEM] * count + [HBM] * len(given),
        out_specs=HBM,
        scratch_shapes=[pltpu.SemaphoreType.DMA((2 * count,))],
        input_output_aliases={count: 0} if given else {},
        compiler_params=params(4),
        name="placed",
    )(*pieces, *given)


def on_device(
    activations,
    cotangent,
    master_weights,
    first_moment,
    second_moment,
    step_count,
    language_ids,
    language_rates,
):
    steps_done = step_count.astype(jnp.float32)
    corr_one = 1.0 - jnp.power(jnp.float32(beta_one), steps_done)
    corr_two = 1.0 - jnp.power(jnp.float32(beta_two), steps_done)
    scale = jnp.concatenate([1.0 / corr_one, 1.0 / corr_two])
    picked = jnp.arange(language_rates.shape[0], dtype=jnp.int32) == language_ids[0]
    rate = base_rate * jnp.sum(jnp.where(picked, language_rates, jnp.float32(0.0)))
    weights = master_weights.T
    rate = rate.reshape(1)
    terms, near_weights = gradient_terms(activations, cotangent, weights)
    new_first, new_second, update, sums = updated(
        terms, weights, first_moment.T, second_moment.T, scale, near_weights
    )
    near_updates = [moved(update, dz=-1), moved(update, dz=1)]
    sums = total_over_devices(sums)
    own = own_step(sums, rate, weights, update, near_updates)
    far = moved(own, dz=2)
    new_master, plus, minus = near_step(
        sums, rate, [weights] + near_weights, [update] + near_updates, own
    )
    pieces = []
    for block in (own, plus, minus):
        pieces += [block, moved(block, dc=1)]
    near = placed((0, 1, 3), pieces)
    new_weights = placed((2,), [far, moved(far, dc=1)], near)
    return (new_master.T, new_first.T, new_second.T, new_weights.T)


def solution(mesh):
    return jax.shard_map(
        on_device,
        mesh=mesh,
        in_specs=(
            P(("dp", "mp"), None),
            P("dp", "mp"),
            P("dp", "mp"),
            P("dp", "mp"),
            P("dp", "mp"),
            P(),
            P(),
            P(),
        ),
        out_specs=(P("dp", "mp"), P("dp", "mp"), P("dp", "mp"), P(None, "mp")),
        check_vma=False,
    )
```

```python
import functools

import jax
import jax.numpy as jnp
from jax import lax
from jax.experimental import pallas as pl
from jax.experimental.pallas import tpu as pltpu
from jax.sharding import PartitionSpec as P

beta_one = 0.9
beta_two = 0.999
epsilon = 1e-06
decay_weight = 0.1
base_rate = 0.25

ROWS = 640
COLS = 320
BLOCK = 128
GROUP = 2 * ROWS


def moved(array, dz=0, dc=0, dx=0, dy=0):
    pairs = []
    for z in range(4):
        for c in range(2):
            for x in range(4):
                for y in range(4):
                    src = (2 * z + c) * 16 + 4 * x + y
                    dst = (2 * ((z + dz) % 4) + (c + dc) % 2) * 16 + 4 * ((x + dx) % 4) + (y + dy) % 4
                    pairs.append((src, dst))
    return lax.ppermute(array, ("dp", "mp"), pairs)


def place():
    d = lax.axis_index("dp")
    m = lax.axis_index("mp")
    return d // 2, d % 2, m // 4, m % 4


HBM = pl.BlockSpec(memory_space=pltpu.HBM)
ANY = pl.BlockSpec(memory_space=pl.ANY)
VMEM = pl.BlockSpec(memory_space=pltpu.VMEM)
SMEM = pl.BlockSpec(memory_space=pltpu.SMEM)


def params(mib):
    return pltpu.CompilerParams(vmem_limit_bytes=mib * 2**20)


def copy_all(copies, sems):
    started = [pltpu.make_async_copy(src, dst, sems.at[k]) for k, (src, dst) in enumerate(copies)]
    for copy in started:
        copy.start()
    for copy in started:
        copy.wait()


def prepare_kernel(act, cot, *refs):
    acts, cots, sems = refs[:4], refs[4:8], refs[8]
    z, c, x, y = place()
    copies = []
    for kz, out in enumerate(acts):
        base = lax.rem(z + kz, 4) * GROUP
        for half, core in enumerate((c, 1 - c)):
            start = pl.multiple_of(base + core * ROWS, 128)
            copies.append((act.at[:, pl.ds(start, ROWS)], out.at[:, pl.ds(half * ROWS, ROWS)]))
    for ky, out in enumerate(cots):
        for dx in range(4):
            start = (4 * lax.rem(x + dx, 4) + lax.rem(y + ky, 4)) * BLOCK
            start = pl.multiple_of(start, 128)
            copies.append((cot.at[:, pl.ds(start, BLOCK)], out.at[:, pl.ds(dx * BLOCK, BLOCK)]))
    copy_all(copies, sems)


def prepare(activations, cotangent_t):
    bf16 = jnp.bfloat16
    return pl.pallas_call(
        prepare_kernel,
        out_shape=[jax.ShapeDtypeStruct((BLOCK, GROUP), bf16)] * 4
        + [jax.ShapeDtypeStruct((COLS, 4 * BLOCK), bf16)] * 4,
        in_specs=[HBM] * 2,
        out_specs=[VMEM] * 8,
        scratch_shapes=[pltpu.SemaphoreType.DMA((24,))],
        compiler_params=params(4),
        name="prepare",
    )(
        pltpu.with_memory_space_constraint(activations, pltpu.HBM),
        pltpu.with_memory_space_constraint(cotangent_t, pltpu.HBM),
    )


def keep_kernel(*refs):
    pass


def kept(arrays):
    count = len(arrays)
    return pl.pallas_call(
        keep_kernel,
        out_shape=[jax.ShapeDtypeStruct(a.shape, a.dtype) for a in arrays],
        in_specs=[ANY] * count,
        out_specs=[ANY] * count,
        input_output_aliases={k: k for k in range(count)},
        compiler_params=params(1),
        name="kept",
    )(*arrays)


def dot(a, b):
    return jnp.dot(a, b, preferred_element_type=jnp.float32)


def near_kernel(z0, zp, zm, x0, xp, xm, *outs):
    acts = jnp.concatenate(
        [x[kz * BLOCK : (kz + 1) * BLOCK, :] for kz in (0, 1, 3) for x in (x0, xp, xm)], axis=0
    )
    for ky, out in enumerate(outs):
        rows = slice(ky * COLS, (ky + 1) * COLS)
        parts = []
        for z in (z0, zm, zp):
            parts += [z[rows, : 2 * BLOCK], z[rows, 3 * BLOCK :]]
        out[...] = dot(jnp.concatenate(parts, axis=1), acts)


def near_product(z0, zp, zm, x0, xp, xm):
    return pl.pallas_call(
        near_kernel,
        out_shape=[jax.ShapeDtypeStruct((COLS, GROUP), jnp.float32)] * 4,
        in_specs=[VMEM] * 6,
        out_specs=[VMEM] * 4,
        compiler_params=params(14),
        name="near_product",
    )(z0, zp, zm, x0, xp, xm)


def middle_kernel(z0, zp, zm, x0, xp, xm, xd0, xd1, *refs):
    del x0, xp, xm
    rhs = jnp.concatenate([xd0[:BLOCK, :], xd0[BLOCK:, :], xd1[BLOCK:, :]], axis=0)
    for ky in range(4):
        rows = slice(ky * COLS, (ky + 1) * COLS)
        parts = [z[rows, 2 * BLOCK : 3 * BLOCK] for z in (z0, zm, zp)]
        refs[4 + ky][...] = refs[ky][...] + dot(jnp.concatenate(parts, axis=1), rhs)


def middle_product(c_near, a_pieces, totals):
    return pl.pallas_call(
        middle_kernel,
        out_shape=[jax.ShapeDtypeStruct((COLS, GROUP), jnp.float32)] * 4,
        in_specs=[VMEM] * 12,
        out_specs=[VMEM] * 4,
        input_output_aliases={8 + k: k for k in range(4)},
        compiler_params=params(14),
        name="middle_product",
    )(*c_near, *a_pieces, *totals)


def far_kernel(order, *refs):
    zd0, zd1, x0, xp, xm, xd0, xd1 = refs[:7]
    count = len(order)
    totals, outs = refs[7 : 7 + count], refs[8 + count : -1]
    refs[-1][...] = refs[7 + count][...]
    last = slice(2 * BLOCK, 3 * BLOCK)
    rhs = jnp.concatenate([x0[last, :], xp[last, :], xd1[:BLOCK, :], xm[last, :]], axis=0)
    for k, ky in enumerate(order):
        far = zd0 if ky < 2 else zd1
        total = totals[k][...] + dot(far[(ky % 2) * COLS : (ky % 2 + 1) * COLS, :], rhs)
        outs[2 * k][...] = total[:, :ROWS]
        outs[2 * k + 1][...] = total[:, ROWS:]


def far_product(order, pieces, totals, also):
    count = len(order)
    outs = pl.pallas_call(
        functools.partial(far_kernel, order),
        out_shape=[jax.ShapeDtypeStruct((COLS, ROWS), jnp.float32)] * (2 * count)
        + [jax.ShapeDtypeStruct(also.shape, also.dtype)],
        in_specs=[VMEM] * (8 + count),
        out_specs=[VMEM] * (2 * count + 1),
        compiler_params=params(14),
        name="far_product",
    )(*pieces, *[totals[ky] for ky in order], also)
    return {ky: (outs[2 * k], outs[2 * k + 1]) for k, ky in enumerate(order)}, outs[-1]


def ring_gather(block, axis):
    half = block.shape[0] // 2
    plus = moved(block, **{axis: -1})
    minus = moved(block, **{axis: 1})
    far_first = moved(plus[:half], **{axis: -1})
    far_second = moved(minus[half:], **{axis: 1})
    return [block, plus, minus, far_first, far_second]


def exchanged(blocks, axis):
    parts = {k: moved(blocks[k], **{axis: k}) for k in (2, 1, 3)}
    return jnp.concatenate([blocks[0], parts[1], parts[2], parts[3]], axis=0)


def gradient_terms(activations, cotangent, weights):
    parts = prepare(activations, cotangent.T)
    c_block = exchanged(parts[4:], "dy")
    a_block = exchanged(kept(parts[:4]), "dz")
    c_pieces = ring_gather(c_block, "dz")
    a_pieces = ring_gather(a_block, "dx")
    totals = near_product(*c_pieces[:3], *a_pieces[:3])
    totals = middle_product(c_pieces[:3], a_pieces, totals)
    far_pieces = c_pieces[3:] + a_pieces
    terms, weights = far_product((2,), far_pieces, totals, weights)
    half = COLS // 2
    far = moved(terms[2][1], dc=1)
    others, weights = far_product((1, 3, 0), far_pieces, totals, weights)
    terms |= others
    low = moved(terms[2][0][:half] + far[:half], dy=-1)
    high = moved(terms[2][0][half:] + far[half:], dy=1)
    down = terms[1][0] + moved(terms[1][1], dc=1)
    up = terms[3][0] + moved(terms[3][1], dc=1)
    own = moved(terms[0][1], dc=1)
    near = [moved(weights, dz=-1), moved(weights, dz=1)]
    down = jnp.concatenate([down[:half] + low, down[half:]], axis=0)
    up = jnp.concatenate([up[:half], up[half:] + high], axis=0)
    return [terms[0][0], own, moved(down, dy=-1), moved(up, dy=1)], near


STRIP = 80


def update_kernel(*refs):
    own0, own1, down, up, weights, first, second, scale = refs[:8]
    new_first, new_second, update, sums, held, sems = refs[10:]
    inv_one, inv_two = scale[0], scale[1]
    half = COLS // 2
    carry = (jnp.zeros((8, ROWS), jnp.float32),) * 2
    copies = []
    for base in (0, half):

        def strip(i, carry):
            rows = pl.ds(base + pl.multiple_of(i * STRIP, STRIP), STRIP)
            g = (own0[rows, :] + own1[rows, :]) + (down[rows, :] + up[rows, :])
            w = weights[rows, :]
            m = beta_one * first[rows, :] + (1.0 - beta_one) * g
            v = beta_two * second[rows, :] + (1.0 - beta_two) * g * g
            u = m * inv_one / (jnp.sqrt(v * inv_two) + epsilon) + decay_weight * w
            held[0, rows, :] = m
            held[1, rows, :] = v
            update[rows, :] = u
            out = []
            for total, term in zip(carry, (w * w, u * u)):
                part = term[:8]
                for k in range(8, STRIP, 8):
                    part = part + term[k : k + 8]
                out.append(total + part)
            return tuple(out)

        carry = lax.fori_loop(0, half // STRIP, strip, carry)
        for k, out in enumerate((new_first, new_second)):
            rows = pl.ds(base, half)
            copies.append(pltpu.make_async_copy(held.at[k, rows], out.at[rows], sems.at[len(copies)]))
            copies[-1].start()
    for k, total in enumerate(carry):
        part = total[:, :128]
        for j in range(128, ROWS, 128):
            part = part + total[:, j : j + 128]
        sums[8 * k : 8 * k + 8, :] = part
    for copy in copies:
        copy.wait()


def updated(terms, weights, first, second, scale, near):
    block = jax.ShapeDtypeStruct((COLS, ROWS), jnp.float32)
    return pl.pallas_call(
        update_kernel,
        out_shape=[block] * 3 + [jax.ShapeDtypeStruct((16, 128), jnp.float32)],
        in_specs=[VMEM] * 7 + [SMEM] + [ANY] * 2,
        out_specs=[HBM] * 2 + [VMEM] * 2,
        scratch_shapes=[
            pltpu.VMEM((2, COLS, ROWS), jnp.float32),
            pltpu.SemaphoreType.DMA((4,)),
        ],
        compiler_params=params(6),
        name="update",
    )(*terms, weights, first, second, scale, *near)


def total_over_devices(values):
    values = values + moved(values, dc=1)
    for axis in ("dx", "dy", "dz"):
        one, two, three = (moved(values, **{axis: k}) for k in (1, 2, 3))
        values = (values + two) + (one + three)
    return values


def scale_of(sums, rate):
    weight_sq = jnp.sum(jnp.sum(sums[:8, :], axis=0, keepdims=True), axis=1, keepdims=True)
    update_sq = jnp.sum(jnp.sum(sums[8:, :], axis=0, keepdims=True), axis=1, keepdims=True)
    return rate[0] * (jnp.sqrt(weight_sq) / jnp.sqrt(update_sq))


def step_kernel(sums, rate, weights, update, near0, near1, new_weights):
    scale = scale_of(sums, rate)

    def strip(i, carry):
        rows = pl.ds(pl.multiple_of(i * STRIP, STRIP), STRIP)
        new_weights[rows, :] = (weights[rows, :] - scale * update[rows, :]).astype(jnp.bfloat16)
        return carry

    lax.fori_loop(0, COLS // STRIP, strip, 0)


def own_step(sums, rate, weights, update, near):
    return pl.pallas_call(
        step_kernel,
        out_shape=jax.ShapeDtypeStruct((COLS, ROWS), jnp.bfloat16),
        in_specs=[VMEM, SMEM, VMEM, VMEM] + [ANY] * 2,
        out_specs=VMEM,
        compiler_params=params(6),
        name="own_step",
    )(sums, rate, weights, update, *near)


def near_step_kernel(sums, rate, w, wp, wm, u, up, um, own, new_master, plus, minus):
    scale = scale_of(sums, rate)

    def strip(i, carry):
        rows = pl.ds(pl.multiple_of(i * STRIP, STRIP), STRIP)
        new_master[rows, :] = w[rows, :] - scale * u[rows, :]
        plus[rows, :] = (wp[rows, :] - scale * up[rows, :]).astype(jnp.bfloat16)
        minus[rows, :] = (wm[rows, :] - scale * um[rows, :]).astype(jnp.bfloat16)
        return carry

    lax.fori_loop(0, COLS // STRIP, strip, 0)


def near_step(sums, rate, weights, updates, own):
    return pl.pallas_call(
        near_step_kernel,
        out_shape=[jax.ShapeDtypeStruct((COLS, ROWS), jnp.float32)]
        + [jax.ShapeDtypeStruct((COLS, ROWS), jnp.bfloat16)] * 2,
        in_specs=[VMEM, SMEM] + [VMEM] * 6 + [ANY],
        out_specs=[VMEM] * 3,
        compiler_params=params(6),
        name="near_step",
    )(sums, rate, *weights, *updates, own)


def place_kernel(offsets, *refs):
    pieces, out, sems = refs[: 2 * len(offsets)], refs[-2], refs[-1]
    z, c, x, y = place()
    copies = []
    for k, dz in enumerate(offsets):
        for half, core in enumerate((c, 1 - c)):
            start = pl.multiple_of((2 * lax.rem(z + dz, 4) + core) * ROWS, 128)
            for first in range(0, COLS, COLS // 2):
                rows = pl.ds(first, COLS // 2)
                copies.append((pieces[2 * k + half].at[rows], out.at[rows, pl.ds(start, ROWS)]))
    copy_all(copies, sems)


def placed(offsets, pieces, held=None):
    count = len(pieces)
    given = [] if held is None else [held]
    return pl.pallas_call(
        functools.partial(place_kernel, offsets),
        out_shape=jax.ShapeDtypeStruct((COLS, 8 * ROWS), jnp.bfloat16),
        in_specs=[VMEM] * count + [HBM] * len(given),
        out_specs=HBM,
        scratch_shapes=[pltpu.SemaphoreType.DMA((2 * count,))],
        input_output_aliases={count: 0} if given else {},
        compiler_params=params(4),
        name="placed",
    )(*pieces, *given)


def on_device(
    activations,
    cotangent,
    master_weights,
    first_moment,
    second_moment,
    step_count,
    language_ids,
    language_rates,
):
    steps_done = step_count.astype(jnp.float32)
    corr_one = 1.0 - jnp.power(jnp.float32(beta_one), steps_done)
    corr_two = 1.0 - jnp.power(jnp.float32(beta_two), steps_done)
    scale = jnp.concatenate([1.0 / corr_one, 1.0 / corr_two])
    picked = jnp.arange(language_rates.shape[0], dtype=jnp.int32) == language_ids[0]
    rate = base_rate * jnp.sum(jnp.where(picked, language_rates, jnp.float32(0.0)))
    weights = master_weights.T
    rate = rate.reshape(1)
    terms, near_weights = gradient_terms(activations, cotangent, weights)
    new_first, new_second, update, sums = updated(
        terms, weights, first_moment.T, second_moment.T, scale, near_weights
    )
    near_updates = [moved(update, dz=-1), moved(update, dz=1)]
    sums = total_over_devices(sums)
    own = own_step(sums, rate, weights, update, near_updates)
    far = moved(own, dz=2)
    new_master, plus, minus = near_step(
        sums, rate, [weights] + near_weights, [update] + near_updates, own
    )
    pieces = []
    for block in (own, plus, minus):
        pieces += [block, moved(block, dc=1)]
    near = placed((0, 1, 3), pieces)
    new_weights = placed((2,), [far, moved(far, dc=1)], near)
    return (new_master.T, new_first.T, new_second.T, new_weights.T)


def solution(mesh):
    return jax.shard_map(
        on_device,
        mesh=mesh,
        in_specs=(
            P(("dp", "mp"), None),
            P("dp", "mp"),
            P("dp", "mp"),
            P("dp", "mp"),
            P("dp", "mp"),
            P(),
            P(),
            P(),
        ),
        out_specs=(P("dp", "mp"), P("dp", "mp"), P("dp", "mp"), P(None, "mp")),
        check_vma=False,
    )
```
